512 devices in a mesh: seq: 128 (over y, z, core), tp: 4 (over x).
Axes of the slice: x: 4, y: 8, z: 8, core: 2. Of those that a mesh axis runs over, the one named last changes fastest.
Arguments:
- queries: bfloat16 [16384, 4096], P('seq', 'tp'), may hold values from -12 to 12
- keys: bfloat16 [16384, 512], P('seq', 'tp'), may hold values from -12 to 12
- values: bfloat16 [16384, 512], P('seq', 'tp'), may hold values from -6 to 6
- sinks: float32 [64], P('tp'), may hold values from 0.5 to 4.5
- session_start: int32 [16384], P('seq'), may hold values from 0 to 16383, as said below
- residual: bfloat16 [16384, 2880], P('seq', 'tp'), may hold values from -40 to 40
- w_out: bfloat16 [4096, 2880], P('seq', 'tp'), may hold values from -0.09375 to 0.09375
- norm_gain: float32 [2880], P('tp'), may hold values from 0.1 to 1.9
- expert_ids: int32 [16384, 4], P('seq'), may hold values from 0 to 63, all different within a row; in each aligned block of 128 rows (0 to 127, 128 to 255, ...) at most 10 rows name the same one
- expert_gates: bfloat16 [16384, 4], P('seq'), may hold values from 0.099609375 to 0.59765625
- w_gate: bfloat16 [2880, 92160], P('tp', 'seq'), may hold values from -0.109375 to 0.109375
- w_up: bfloat16 [2880, 92160], P('tp', 'seq'), may hold values from -0.109375 to 0.109375
- w_down: bfloat16 [92160, 2880], P('seq', 'tp'), may hold values from -0.15625 to 0.15625
Outputs:
- layer_out: bfloat16 [16384, 2880], P('seq', 'tp')
The draws below stay inside these ranges and needn't reach their ends.
Inputs may be any that keep to these rules, and one draw needn't show every extreme that they name: `expert_ids`: each row names 4 different experts. Within the rows of one seq index (aligned blocks of 128 rows) no expert is named by more than 10 rows, a bound that some block reaches. `session_start`: nondecreasing; each entry is the first position of its token's session, so session_start[i] <= i, with equality at a session's first token.
All inputs are finite; a program needn't handle non-finite values.
Results may differ from the reference program's by a relative error of at most 0.013.
Values may be sent and summed in bfloat16 or wider, within the bound.
No kernel may reach another device: no remote copies, remote signals or barrier semaphores. Data moves between devices by JAX's collectives and lax.ppermute only.
A program may use at most 64 MiB of HBM per device.

```python
import math
import jax
import jax.numpy as jnp
import numpy as np
from jax import lax

D = 2880
QUERY_HEADS = 64
KEY_VALUE_HEADS = 8
HEAD_SIZE = 64
WINDOW_SPAN = 128
HID = 1440
TOP = 4
TOKENS_PER_SHARD = 128
TOTAL_TOKENS = 16384
EXPERTS = 64
CAP = 10
N_SEQ = 128
N_TP = 4


def query_key_pair(key):
    random_base_key = jax.random.fold_in(key, 17)
    unrotated_keys = jnp.clip(jax.random.normal(jax.random.fold_in(random_base_key, 1), (TOTAL_TOKENS, KEY_VALUE_HEADS * HEAD_SIZE), jnp.float32), -6.0, 6.0)
    queries_raw = jnp.clip(jax.random.normal(jax.random.fold_in(random_base_key, 2), (TOTAL_TOKENS, QUERY_HEADS * HEAD_SIZE), jnp.float32), -6.0, 6.0)
    return (queries_raw, unrotated_keys)


def draw_queries(key, part):
    queries_raw, unrotated_keys = query_key_pair(key)
    return queries_raw.astype(jnp.bfloat16)


def draw_keys(key, part):
    queries_raw, unrotated_keys = query_key_pair(key)
    return unrotated_keys.astype(jnp.bfloat16)


def draw_session_start(key, part):
    markers = jax.random.randint(jax.random.fold_in(key, 31), (TOTAL_TOKENS,), 0, 48)
    positions = jnp.arange(TOTAL_TOKENS, dtype=jnp.int32)
    begins = (markers == 0) | (positions == 0)
    return lax.cummax(jnp.where(begins, positions, 0), axis=0).astype(jnp.int32)


def draw_residual(key, part):
    random_base_key = jax.random.fold_in(key, 41)
    column_pos = jnp.arange(D, dtype=jnp.float32) / D
    column_scale = jnp.exp(jnp.log(4.0) * column_pos) * jnp.exp(jax.random.uniform(jax.random.fold_in(random_base_key, 1), (D,), jnp.float32, 0.0, jnp.log(3.0))) / 4.0
    row_scale = jnp.exp(jax.random.uniform(jax.random.fold_in(random_base_key, 2), (TOTAL_TOKENS, 1), jnp.float32, 0.0, jnp.log(10.0))) / 5.0
    entries = jnp.clip(jax.random.normal(jax.random.fold_in(random_base_key, 3), (TOTAL_TOKENS, D), jnp.float32), -6.0, 6.0)
    return (entries * row_scale * column_scale[None, :]).astype(jnp.bfloat16)


def level_of(rng, dims, pieces, low, high):
    def one(dim, blocks):
        draws = jax.random.uniform(jax.random.fold_in(jax.random.fold_in(rng, 6), dim), (blocks,), jnp.float32, low / len(pieces), high / len(pieces))
        return jnp.repeat(jnp.exp(draws), dims[dim] // blocks).reshape((-1,) + (1,) * (len(dims) - dim - 1))

    loudness = one(*pieces[0])
    for cut in pieces[1:]:
        loudness = loudness * one(*cut)
    return loudness


def assign_block(rng, own, number, rows, amount, top, limit, skew):
    ranking = jax.random.permutation(rng, amount)
    packed, common = portions_of(amount, rows * top, limit, skew, True), portions_of(amount, rows * top, limit, skew, False)
    places = jnp.arange(amount)

    def named(lengths, rotation):
        used = int((lengths > 0).sum())
        fixed = max(1, used // 4)
        moved = fixed + (places - fixed + rotation * (used - fixed)) % max(1, amount - fixed)
        return jnp.zeros((amount,), jnp.int32).at[ranking[jnp.where(places < fixed, places, moved)]].set(jnp.asarray(lengths, jnp.int32))

    lengths = jnp.where(number % 4 == 0, named(packed, number // 4), named(common, number - number // 4 - 1))
    mixed = jax.random.permutation(jax.random.fold_in(own, 3), amount)
    giver, receiver = mixed[0:amount // 2 * 2:2], mixed[1:amount // 2 * 2:2]
    slack = jnp.minimum(lengths[giver] - 1, limit - lengths[receiver]) // 2
    slack = jnp.where((giver == ranking[0]) | (receiver == ranking[0]) | (lengths[receiver] == 0), 0, jnp.maximum(slack, 0))
    moved = jax.random.randint(jax.random.fold_in(own, 4), (amount // 2,), 0, 1 << 20) % (slack + 1)
    lengths = lengths.at[giver].add(-moved).at[receiver].add(moved)
    members = jnp.searchsorted(jnp.cumsum(lengths), jnp.arange(rows * top), side="right").astype(jnp.int32)
    listing = members.reshape(top, rows).T
    listing = listing[jax.random.permutation(jax.random.fold_in(own, 1), rows)]
    rotation = jax.random.randint(jax.random.fold_in(own, 2), (rows, 1), 0, top)
    return jnp.take_along_axis(listing, (jnp.arange(top)[None, :] + rotation) % top, axis=1)


def portions_of(number_of, total, limit, skew, full):
    loads = [(1 << 20) // math.isqrt(standing ** skew) + 1 for standing in range(1, number_of + 1)]
    largest = limit if full else min(limit, max(-(-total // number_of), total * loads[0] // sum(loads)))
    least = 1 if total - largest >= number_of - 1 else 0
    holding, spare = [largest] + [least] * (number_of - 1), total - largest - least * (number_of - 1)
    while spare > 0:
        free = [i for i in range(1, number_of) if holding[i] < largest] or [i for i in range(1, number_of) if holding[i] < limit]
        whole, budget = sum([loads[i] for i in free]), spare
        for i in free:
            addition = min(limit - holding[i], max(1, budget * loads[i] // whole), spare)
            holding[i] = holding[i] + addition
            spare = spare - addition
    return np.array(holding)


def bell_draw(rng, shape, deviation, limit, split=(), held_as=jnp.bfloat16):
    values = deviation * jax.random.normal(rng, shape, jnp.float32)
    if split:
        values = values * level_of(rng, shape, split, -0.22, 0.18)
    return jnp.clip(values, -limit, limit).astype(held_as)


def setup_inputs(seed: int = 0) -> dict:
    key_of = jax.random.split(jax.random.key(seed), 14)
    queries = draw_queries(jax.random.fold_in(key_of[13], 71), 0)
    keys = draw_keys(jax.random.fold_in(key_of[13], 71), 0)
    values = bell_draw(key_of[2], (TOTAL_TOKENS, KEY_VALUE_HEADS * HEAD_SIZE), 1.0, 6.0, ((0, 128), (1, 4)))
    sinks = jnp.clip(0.5 + 4.0 * jax.random.uniform(key_of[3], (QUERY_HEADS,), jnp.float32) ** level_of(key_of[3], (QUERY_HEADS,), ((0, 4),), -0.2, 0.2), 0.5, 4.5)
    session_start = draw_session_start(jax.random.fold_in(key_of[13], 71), 0)
    residual = draw_residual(jax.random.fold_in(key_of[13], 71), 0)
    w_out = bell_draw(key_of[6], (QUERY_HEADS * HEAD_SIZE, D), (QUERY_HEADS * HEAD_SIZE) ** -0.5, 0.09375, ((0, 128), (1, 4)))
    norm_gain = jnp.clip(1.0 + 0.18 * jax.random.normal(key_of[7], (D,), jnp.float32), 0.1, 1.9)
    expert_ids_keys = jax.random.split(jax.random.fold_in(key_of[8], 1), TOTAL_TOKENS // TOKENS_PER_SHARD)
    expert_ids_turns = jax.random.permutation(jax.random.fold_in(key_of[8], 3), TOTAL_TOKENS // TOKENS_PER_SHARD)
    expert_ids = jax.vmap(lambda own, number: assign_block(jax.random.fold_in(key_of[8], 2), own, number, TOKENS_PER_SHARD, EXPERTS, TOP, CAP, 2))(expert_ids_keys, expert_ids_turns).reshape((TOTAL_TOKENS, TOP))
    expert_gates = jnp.clip(0.099609375 + 0.49804688 * jax.random.uniform(key_of[9], (TOTAL_TOKENS, TOP), jnp.float32) ** level_of(key_of[9], (TOTAL_TOKENS, TOP), ((0, 128),), -0.2, 0.2), 0.099609375, 0.59765625).astype(jnp.bfloat16)
    w_gate = bell_draw(key_of[10], (D, EXPERTS * HID), D ** -0.5, 0.109375, ((0, 4), (1, 128)))
    w_up = bell_draw(key_of[11], (D, EXPERTS * HID), D ** -0.5, 0.109375, ((0, 4), (1, 128)))
    w_down = bell_draw(key_of[12], (EXPERTS * HID, D), HID ** -0.5, 0.15625, ((0, 128), (1, 4)))
    return dict(queries=queries, keys=keys, values=values, sinks=sinks, session_start=session_start, residual=residual, w_out=w_out, norm_gain=norm_gain, expert_ids=expert_ids, expert_gates=expert_gates, w_gate=w_gate, w_up=w_up, w_down=w_down)


NEGATIVE = -1e+30
EPSILON = 1e-05

def attend_block(block, queries, keys_pad, values_pad, sinks, session_start):
    offset = (block * TOKENS_PER_SHARD).astype(jnp.int32)
    query_groups = QUERY_HEADS // KEY_VALUE_HEADS
    query_row_matrix = lax.dynamic_slice_in_dim(queries, offset, TOKENS_PER_SHARD, 0)
    key_row_matrix = lax.dynamic_slice_in_dim(keys_pad, offset, TOKENS_PER_SHARD + WINDOW_SPAN, 0)
    value_row_matrix = lax.dynamic_slice_in_dim(values_pad, offset, TOKENS_PER_SHARD + WINDOW_SPAN, 0)
    starts = lax.dynamic_slice_in_dim(session_start, offset, TOKENS_PER_SHARD, 0)
    query_pos = offset + jnp.arange(TOKENS_PER_SHARD, dtype=jnp.int32)
    key_pos = offset - WINDOW_SPAN + jnp.arange(TOKENS_PER_SHARD + WINDOW_SPAN, dtype=jnp.int32)
    distance = query_pos[:, None] - key_pos[None, :]
    allowed = (distance >= 0) & (distance < WINDOW_SPAN) & (key_pos[None, :] >= starts[:, None])
    blocked_queries = query_row_matrix.reshape(TOKENS_PER_SHARD, KEY_VALUE_HEADS, query_groups, HEAD_SIZE).astype(jnp.float32)
    blocked_keys = key_row_matrix.reshape(TOKENS_PER_SHARD + WINDOW_SPAN, KEY_VALUE_HEADS, HEAD_SIZE).astype(jnp.float32)
    blocked_values = value_row_matrix.reshape(TOKENS_PER_SHARD + WINDOW_SPAN, KEY_VALUE_HEADS, HEAD_SIZE).astype(jnp.float32)
    scores = jnp.einsum('qhgd,khd->hgqk', blocked_queries, blocked_keys) * HEAD_SIZE ** (-0.5)
    scores = jnp.where(allowed[None, None], scores, NEGATIVE)
    sink_column = sinks.reshape(KEY_VALUE_HEADS, query_groups)[:, :, None, None]
    row_max = jnp.maximum(lax.optimization_barrier(jnp.max(scores, axis=-1, keepdims=True)), sink_column)
    numerator = jnp.exp(scores - row_max) * allowed[None, None].astype(jnp.float32)
    denominator = lax.optimization_barrier(jnp.sum(numerator, axis=-1, keepdims=True)) + jnp.exp(sink_column - row_max)
    weights = (numerator / denominator).astype(jnp.bfloat16)
    head_out = jnp.einsum('hgqk,khd->qhgd', weights.astype(jnp.float32), blocked_values)
    return head_out.astype(jnp.bfloat16).reshape(TOKENS_PER_SHARD, QUERY_HEADS * HEAD_SIZE)

def reference(queries, keys, values, sinks, session_start, residual, w_out, norm_gain, expert_ids, expert_gates, w_gate, w_up, w_down):
    padding_rows = jnp.zeros((WINDOW_SPAN, KEY_VALUE_HEADS * HEAD_SIZE), jnp.bfloat16)
    keys_pad = jnp.concatenate([padding_rows, keys], axis=0)
    values_pad = jnp.concatenate([padding_rows, values], axis=0)
    head_blocks = lax.map(lambda block: attend_block(block, queries, keys_pad, values_pad, sinks, session_start), jnp.arange(N_SEQ, dtype=jnp.int32))
    head_all = head_blocks.reshape(TOTAL_TOKENS, QUERY_HEADS * HEAD_SIZE)
    attended = jnp.dot(head_all, w_out, preferred_element_type=jnp.float32)
    stream = residual.astype(jnp.float32) + attended
    squares = lax.optimization_barrier(jnp.sum(stream * stream, axis=1)) / D
    normed = (stream * lax.rsqrt(squares + EPSILON)[:, None] * norm_gain[None, :]).astype(jnp.bfloat16)
    present = expert_ids[:, :, None] == jnp.arange(EXPERTS, dtype=jnp.int32)[None, None, :]
    per_row = lax.optimization_barrier(jnp.sum(present.astype(jnp.int32), axis=1))
    block_rows = per_row.reshape(N_SEQ, TOKENS_PER_SHARD, EXPERTS)
    before = (jnp.cumsum(block_rows, axis=1) - block_rows).reshape(TOTAL_TOKENS, EXPERTS)
    position = lax.optimization_barrier(jnp.sum(jnp.where(present, before[:, None, :], 0), axis=2)).astype(jnp.int32)
    token_ids = jnp.arange(TOTAL_TOKENS, dtype=jnp.int32)
    slot_index = ((token_ids // TOKENS_PER_SHARD)[:, None] * CAP + position).astype(jnp.int32)
    token_grid = jnp.broadcast_to(token_ids[:, None], (TOTAL_TOKENS, TOP)).astype(jnp.int32)
    slot_table = jnp.full((EXPERTS, N_SEQ * CAP), -1, jnp.int32).at[expert_ids, slot_index].set(token_grid)
    gate_table = jnp.zeros((EXPERTS, N_SEQ * CAP), jnp.float32).at[expert_ids, slot_index].set(expert_gates.astype(jnp.float32))
    quarter = D // N_TP
    half_hid = HID // 2

    def one_expert(running, expert):
        slot_token = slot_table[expert]
        filled = slot_token >= 0
        safe_token = jnp.maximum(slot_token, 0).astype(jnp.int32)
        expert_rows = jnp.where(filled[:, None], normed[safe_token], jnp.zeros((), jnp.bfloat16))
        gate_cols = lax.dynamic_slice_in_dim(w_gate, (expert * HID).astype(jnp.int32), HID, 1)
        up_cols = lax.dynamic_slice_in_dim(w_up, (expert * HID).astype(jnp.int32), HID, 1)
        gate_sum = jnp.zeros((N_SEQ * CAP, HID), jnp.float32)
        up_sum = jnp.zeros((N_SEQ * CAP, HID), jnp.float32)
        for portion in range(N_TP):
            row_part = expert_rows[:, portion * quarter:(portion + 1) * quarter]
            gate_piece = jnp.dot(row_part, gate_cols[portion * quarter:(portion + 1) * quarter], preferred_element_type=jnp.float32)
            up_piece = jnp.dot(row_part, up_cols[portion * quarter:(portion + 1) * quarter], preferred_element_type=jnp.float32)
            gate_sum = gate_sum + lax.optimization_barrier(gate_piece.astype(jnp.bfloat16)).astype(jnp.float32)
            up_sum = up_sum + lax.optimization_barrier(up_piece.astype(jnp.bfloat16)).astype(jnp.float32)
        active = (jax.nn.silu(gate_sum) * up_sum).astype(jnp.bfloat16)
        down_rows = lax.dynamic_slice_in_dim(w_down, (expert * HID).astype(jnp.int32), HID, 0)
        first_half = jnp.dot(active[:, :half_hid], down_rows[:half_hid], preferred_element_type=jnp.float32).astype(jnp.bfloat16)
        second_half = jnp.dot(active[:, half_hid:], down_rows[half_hid:], preferred_element_type=jnp.float32).astype(jnp.bfloat16)
        paired = (first_half.astype(jnp.float32) + second_half.astype(jnp.float32)).astype(jnp.bfloat16)
        combined = lax.optimization_barrier(paired).astype(jnp.float32)
        contrib = gate_table[expert][:, None] * combined
        running = running.at[safe_token].add(jnp.where(filled[:, None], contrib, jnp.zeros((), jnp.float32)))
        return (running, None)
    moe, _ = lax.scan(one_expert, jnp.zeros((TOTAL_TOKENS, D), jnp.float32), jnp.arange(EXPERTS, dtype=jnp.int32))
    return (stream + moe).astype(jnp.bfloat16)
```

```python
import jax
import jax.numpy as jnp
from jax import lax
from jax.experimental import pallas as pl
from jax.experimental.pallas import tpu as pltpu
from jax.sharding import Mesh, PartitionSpec as P

D = 2880
HEAD = 64
HALF = 32
GROUPS = 8
WINDOW = 128
EXPERTS = 64
TP = 4
QUARTER = 720
PADDED = 768
BLOCKS = 24
CLASS_SLOTS = 3
SLOTS = EXPERTS * CLASS_SLOTS
EPSILON = 1e-05
NEGATIVE = -1e30
F32 = jnp.float32
BF16 = jnp.bfloat16
SEQ = ("y", "z", "core")
CHIPS = ("y", "z")


def shifted(block, axis, distance):
    size = lax.axis_size(axis)
    return lax.ppermute(block, axis, [(i, (i + distance) % size) for i in range(size)])


def call(kernel, out_shape, args, scratch=(), spaces=None, flops=0, moved=0):
    spaces = spaces or [pltpu.VMEM] * len(args)
    return pl.pallas_call(
        kernel,
        out_shape=out_shape,
        in_specs=[pl.BlockSpec(memory_space=s) for s in spaces],
        out_specs=jax.tree.map(lambda _: pl.BlockSpec(memory_space=pltpu.VMEM), out_shape),
        scratch_shapes=list(scratch),
        cost_estimate=pl.CostEstimate(flops=flops, bytes_accessed=moved, transcendentals=0),
        compiler_params=pltpu.CompilerParams(vmem_limit_bytes=48 * 1024 * 1024),
    )(*args)


def attention_kernel(q_ref, own_ref, before_ref, start_ref, sink_ref, out_ref):
    rows = q_ref.shape[0]
    i = lax.broadcasted_iota(jnp.int32, (rows, rows), 0)
    j = lax.broadcasted_iota(jnp.int32, (rows, rows), 1)
    start = start_ref[...]
    allowed_before = (j > i) & (j >= start)
    allowed_own = (j <= i) & (j + WINDOW >= start)
    row = lax.broadcasted_iota(jnp.int32, (2 * HEAD, GROUPS * HALF), 0)
    col = lax.broadcasted_iota(jnp.int32, (2 * HEAD, GROUPS * HALF), 1)
    group_of_lane = lax.broadcasted_iota(jnp.int32, (rows, GROUPS * HALF), 1) // HALF
    contract = (((1,), (1,)), ((), ()))
    for h in range(2):
        lanes = slice(h * HEAD, (h + 1) * HEAD)
        k_own, k_before = own_ref[:, lanes], before_ref[:, lanes]
        spread = []
        for c in range(2):
            pick = (row == h * HEAD + c * HALF + col % HALF).astype(BF16)
            spread.append(
                [
                    jnp.dot(ref[:, 2 * HEAD :], pick, preferred_element_type=F32).astype(BF16)
                    for ref in (before_ref, own_ref)
                ]
            )
        totals = [jnp.zeros((rows, GROUPS * HALF), F32) for _ in range(2)]
        for g in range(GROUPS):
            head = h * GROUPS + g
            q = q_ref[:, head * HEAD : (head + 1) * HEAD]
            s_before = lax.dot_general(q, k_before, contract, preferred_element_type=F32)
            s_own = lax.dot_general(q, k_own, contract, preferred_element_type=F32)
            s_before = jnp.where(allowed_before, s_before * HEAD**-0.5, NEGATIVE)
            s_own = jnp.where(allowed_own, s_own * HEAD**-0.5, NEGATIVE)
            sink = sink_ref[head]
            top = jnp.max(jnp.maximum(s_before, s_own), axis=1, keepdims=True)
            top = jnp.maximum(top, sink)
            e_before = jnp.exp(s_before - top)
            e_own = jnp.exp(s_own - top)
            total = jnp.sum(e_before + e_own, axis=1, keepdims=True) + jnp.exp(sink - top)
            p_before = (e_before / total).astype(BF16)
            p_own = (e_own / total).astype(BF16)
            for c in range(2):
                v_before, v_own = spread[c]
                zero = jnp.zeros_like(v_own)
                mine = group_of_lane == g
                totals[c] += jnp.dot(
                    p_before, jnp.where(mine, v_before, zero), preferred_element_type=F32
                ) + jnp.dot(p_own, jnp.where(mine, v_own, zero), preferred_element_type=F32)
        for c in range(2):
            made = totals[c].astype(BF16)
            for t in range(TP):
                out_ref[c, t, h] = made


def projection_kernel(index_ref, heads_ref, *refs):
    shards, (own_ref, other_ref, total) = refs[:9], refs[9:]
    me = index_ref[8]
    rows = own_ref.shape[0]
    for half in range(2):
        acc = jnp.zeros((rows, QUARTER), F32)
        for n in range(7):
            chunk = heads_ref[half, index_ref[n]]
            acc += jnp.dot(chunk, shards[n][...], preferred_element_type=F32)
        chunk = heads_ref[half, index_ref[7]]
        depth = chunk.shape[1] // 2
        acc += jnp.dot(chunk[:, :depth], shards[7][...], preferred_element_type=F32)
        acc += jnp.dot(chunk[:, depth:], shards[8][...], preferred_element_type=F32)
        total[half] = acc
    own_ref[...] = total[me]
    other_ref[...] = total[1 - me]


def stream_kernel(residual_ref, own_ref, got_ref, gain_ref, stream_ref, rows_ref):
    stream = residual_ref[...].astype(F32) + (own_ref[...] + got_ref[...])
    stream_ref[...] = stream
    squares = jnp.sum(stream * stream, axis=1, keepdims=True)
    scaled = (stream * gain_ref[...]).astype(BF16)
    lane = lax.broadcasted_iota(jnp.int32, (stream.shape[0], PADDED - QUARTER), 1)
    high = squares.astype(BF16).astype(F32)
    middle = (squares - high).astype(BF16).astype(F32)
    low = squares - high - middle
    extra = jnp.where(lane == 0, high, jnp.where(lane == 1, middle, jnp.where(lane == 2, low, 0.0)))
    extra = extra.astype(BF16)
    for t in range(TP):
        rows_ref[t, :, :QUARTER] = scaled
        rows_ref[t, :, QUARTER:] = extra


def dispatch_kernel(rows_ref, routing_ref, out_ref, flat):
    squares = jnp.zeros((rows_ref.shape[1], 1), F32)
    for t in range(TP):
        squares += jnp.sum(rows_ref[t, :, QUARTER:].astype(F32), axis=1, keepdims=True)
    scale = lax.rsqrt(squares / D + EPSILON)
    routing = routing_ref[...]
    for t in range(TP):
        normed = (rows_ref[t].astype(F32) * scale).astype(BF16)
        picked = jnp.dot(routing, normed, preferred_element_type=F32)
        for b in range(6):
            flat[pl.ds(t * 6 + b, SLOTS, stride=BLOCKS), :] = picked[:, b * 128 : (b + 1) * 128]
    out_ref[...] = flat[...].astype(BF16)


def expert_kernel(mine_ref, other_ref, weights_ref, to_mine_ref, to_other_ref, flat, rows, w, sem):
    copies = [pltpu.make_async_copy(weights_ref.at[t], w.at[t], sem.at[t]) for t in range(TP)]
    for copy in copies:
        copy.start()
    for n, ref in enumerate((mine_ref, other_ref)):
        flat[...] = ref[...].astype(F32)
        for b in range(BLOCKS):
            rows[n * SLOTS : (n + 1) * SLOTS, b * 128 : (b + 1) * 128] = flat[
                pl.ds(b, SLOTS, stride=BLOCKS), :
            ].astype(BF16)
    gate = jnp.zeros((2 * SLOTS, QUARTER), F32)
    up = jnp.zeros((2 * SLOTS, QUARTER), F32)
    for t in range(TP):
        copies[t].wait()
        part = rows[:, t * PADDED : t * PADDED + QUARTER]
        gate += jnp.dot(part, w[t, :QUARTER, :], preferred_element_type=F32)
        up += jnp.dot(part, w[t, QUARTER : 2 * QUARTER, :], preferred_element_type=F32)
    active = (gate / (1.0 + jnp.exp(-gate)) * up).astype(BF16)
    for n, ref in enumerate((to_mine_ref, to_other_ref)):
        part = active[n * SLOTS : (n + 1) * SLOTS]
        for t in range(TP):
            made = jnp.dot(part, w[t, 2 * QUARTER :, :], preferred_element_type=F32)
            made = jnp.concatenate([made, jnp.zeros((SLOTS, PADDED - QUARTER), F32)], axis=1)
            for b in range(6):
                flat[pl.ds(t * 6 + b, SLOTS, stride=BLOCKS), :] = made[:, b * 128 : (b + 1) * 128]
        ref[...] = flat[...].astype(BF16)


def combine_kernel(back_ref, mixing_ref, out_ref, flat):
    flat[...] = back_ref[...].astype(F32)
    mixing = mixing_ref[...]
    for t in range(TP):
        for b in range(6):
            part = flat[pl.ds(t * 6 + b, SLOTS, stride=BLOCKS), :].astype(BF16)
            out_ref[t, :, b * 128 : (b + 1) * 128] = jnp.dot(
                mixing, part, preferred_element_type=F32
            ).astype(BF16)


def shards(
    queries,
    keys,
    values,
    sinks,
    session_start,
    residual,
    w_out,
    norm_gain,
    expert_ids,
    expert_gates,
    w_gate,
    w_up,
    w_down,
):
    count = queries.shape[0]
    y, core, tp = lax.axis_index("y"), lax.axis_index("core"), lax.axis_index("tp")
    seq_index = lax.axis_index(SEQ)
    seq_size = lax.axis_size("y") * lax.axis_size("z") * lax.axis_size("core")
    y_size, z_size = lax.axis_size("y"), lax.axis_size("z")

    with jax.named_scope("expert_weights"):
        blocks = jnp.concatenate([w_gate, w_up, w_down], axis=0)
        weights = lax.all_gather(blocks, "tp", axis=0, tiled=False)

    with jax.named_scope("projection_rows"):
        spread = jnp.broadcast_to(w_out[None], (z_size,) + w_out.shape)
        column = lax.all_to_all(spread, "z", 0, 0, tiled=True)
        column = column.reshape(z_size * w_out.shape[0], QUARTER)
        half = column.shape[0] // 2
        ahead, behind, pieces = column, column, [column]
        for _ in range(y_size // 2 - 1):
            ahead, behind = shifted(ahead, "y", 1), shifted(behind, "y", -1)
            pieces += [ahead, behind]
        pieces += [shifted(ahead[:half], "y", 1), shifted(behind[half:], "y", -1)]
        sources = [y]
        for k in range(1, y_size // 2):
            sources += [(y - k) % y_size, (y + k) % y_size]
        sources.append((y + y_size // 2) % y_size)
        index = jnp.stack([jnp.asarray(v, jnp.int32) for v in sources + [core]])

    with jax.named_scope("attention"):
        pair = jnp.concatenate([keys, values], axis=1)
        before = lax.ppermute(pair, SEQ, [(i, i + 1) for i in range(seq_size - 1)])
        start = (session_start - seq_index * count + WINDOW)[:, None]
        heads = call(
            attention_kernel,
            jax.ShapeDtypeStruct((2, TP, 2, count, GROUPS * HALF), BF16),
            (queries, pair, before, start, sinks),
            spaces=[pltpu.VMEM] * 4 + [pltpu.SMEM],
            flops=2_000_000_000,
            moved=2_000_000,
        )
        heads = lax.all_to_all(
            heads.reshape(2 * TP, 2, count, GROUPS * HALF), ("core", "tp"), 0, 0, tiled=True
        )
        heads = heads.reshape(2, TP * 2, count, GROUPS * HALF)

    with jax.named_scope("stream"):
        own, other = call(
            projection_kernel,
            [jax.ShapeDtypeStruct((count, QUARTER), F32)] * 2,
            (index, heads, *pieces),
            scratch=[pltpu.VMEM((2, count, QUARTER), F32)],
            spaces=[pltpu.SMEM] + [pltpu.VMEM] * 10,
            flops=800_000_000,
            moved=4_000_000,
        )
        got = shifted(other, "core", 1)
        stream, scaled = call(
            stream_kernel,
            [
                jax.ShapeDtypeStruct((count, QUARTER), F32),
                jax.ShapeDtypeStruct((TP, count, PADDED), BF16),
            ],
            (residual, own, got, norm_gain[None, :]),
        )
        scaled = lax.all_to_all(scaled, "tp", 0, 0, tiled=True)

    with jax.named_scope("routing"):
        present = expert_ids[:, :, None] == jnp.arange(EXPERTS, dtype=jnp.int32)[None, None, :]
        per_row = jnp.sum(present.astype(jnp.int32), axis=1)
        earlier = jnp.cumsum(per_row, axis=0) - per_row
        position = jnp.sum(jnp.where(present, earlier[:, None, :], 0), axis=2)
        target = jnp.where(
            position % TP == tp, expert_ids * CLASS_SLOTS + position // TP, -1
        )
        slots = jnp.arange(SLOTS, dtype=jnp.int32)
        routing = jnp.sum((slots[:, None, None] == target[None]).astype(BF16), axis=2)
        mixing = jnp.sum(
            jnp.where(
                slots[None, :, None] == target[:, None, :],
                expert_gates[:, None, :],
                jnp.zeros((), BF16),
            ),
            axis=2,
        )

    flat_scratch = pltpu.VMEM((SLOTS * BLOCKS, 128), F32)
    block = (EXPERTS, CLASS_SLOTS * BLOCKS, 128)
    flat_shape = jax.ShapeDtypeStruct((SLOTS * BLOCKS, 128), BF16)
    with jax.named_scope("dispatch"):
        sending = call(dispatch_kernel, flat_shape, (scaled, routing), scratch=[flat_scratch])
        arrived = lax.all_to_all(sending.reshape(block), CHIPS, 0, 0, tiled=True)
        partner = shifted(arrived, "core", 1)

    with jax.named_scope("experts"):
        to_mine, to_other = call(
            expert_kernel,
            [flat_shape] * 2,
            (arrived.reshape(flat_shape.shape), partner.reshape(flat_shape.shape), weights),
            scratch=[
                flat_scratch,
                pltpu.VMEM((2 * SLOTS, TP * PADDED), BF16),
                pltpu.VMEM((TP, 3 * QUARTER, QUARTER), BF16),
                pltpu.SemaphoreType.DMA((TP,)),
            ],
            spaces=[pltpu.VMEM] * 2 + [pl.ANY],
            flops=5_000_000_000,
            moved=15_000_000,
        )
        received = shifted(to_other, "core", 1)
        both = (to_mine.astype(F32) + received.astype(F32)).astype(BF16)

    with jax.named_scope("combine"):
        back = lax.all_to_all(both.reshape(block), CHIPS, 0, 0, tiled=True)
        mixed = call(
            combine_kernel,
            jax.ShapeDtypeStruct((TP, count, PADDED), BF16),
            (back.reshape(flat_shape.shape), mixing),
            scratch=[flat_scratch],
        )
        mixed = lax.all_to_all(mixed, "tp", 0, 0, tiled=True)
        moe = jnp.sum(mixed[:, :, :QUARTER].astype(F32), axis=0)
        return (stream + moe).astype(BF16)


def solution(mesh):
    whole = Mesh(mesh.devices.reshape(8, 8, 2, 4), ("y", "z", "core", "tp"))
    return jax.shard_map(
        shards,
        mesh=whole,
        in_specs=(
            P(SEQ, "tp"),
            P(SEQ, "tp"),
            P(SEQ, "tp"),
            P("tp"),
            P(SEQ),
            P(SEQ, "tp"),
            P(SEQ, "tp"),
            P("tp"),
            P(SEQ, None),
            P(SEQ, None),
            P("tp", SEQ),
            P("tp", SEQ),
            P(SEQ, "tp"),
        ),
        out_specs=P(SEQ, "tp"),
        check_vma=False,
    )
```

```python
import jax
import jax.numpy as jnp
from jax import lax
from jax.experimental import pallas as pl
from jax.experimental.pallas import tpu as pltpu
from jax.sharding import Mesh, PartitionSpec as P

D = 2880
HEAD = 64
HALF = 32
GROUPS = 8
WINDOW = 128
EXPERTS = 64
TP = 4
QUARTER = 720
PADDED = 768
BLOCKS = 24
FAR = QUARTER + 384
CLASS_SLOTS = 3
SLOTS = EXPERTS * CLASS_SLOTS
EPSILON = 1e-05
NEGATIVE = -1e30
F32 = jnp.float32
BF16 = jnp.bfloat16
SEQ = ("y", "z", "core")
CHIPS = ("y", "z")
GATHERED = ("y", "core")


def shifted(block, axis, distance):
    size = lax.axis_size(axis)
    return lax.ppermute(block, axis, [(i, (i + distance) % size) for i in range(size)])


def call(kernel, out_shape, args, scratch=(), spaces=None, flops=0, moved=0, limit=32):
    spaces = spaces or [pltpu.VMEM] * len(args)
    return pl.pallas_call(
        kernel,
        out_shape=out_shape,
        in_specs=[pl.BlockSpec(memory_space=s) for s in spaces],
        out_specs=jax.tree.map(lambda _: pl.BlockSpec(memory_space=pltpu.VMEM), out_shape),
        scratch_shapes=list(scratch),
        cost_estimate=pl.CostEstimate(flops=flops, bytes_accessed=moved, transcendentals=0),
        compiler_params=pltpu.CompilerParams(vmem_limit_bytes=limit * 1024 * 1024),
    )(*args)


def attention_kernel(q_ref, own_ref, before_ref, start_ref, sink_ref, out_ref):
    rows = q_ref.shape[0]
    i = lax.broadcasted_iota(jnp.int32, (rows, rows), 0)
    j = lax.broadcasted_iota(jnp.int32, (rows, rows), 1)
    start = start_ref[...]
    allowed_before = (j > i) & (j >= start)
    allowed_own = (j <= i) & (j + WINDOW >= start)
    row = lax.broadcasted_iota(jnp.int32, (2 * HEAD, GROUPS * HALF), 0)
    col = lax.broadcasted_iota(jnp.int32, (2 * HEAD, GROUPS * HALF), 1)
    group_of_lane = lax.broadcasted_iota(jnp.int32, (rows, GROUPS * HALF), 1) // HALF
    contract = (((1,), (1,)), ((), ()))
    for h in range(2):
        lanes = slice(h * HEAD, (h + 1) * HEAD)
        k_own, k_before = own_ref[:, lanes], before_ref[:, lanes]
        spread = []
        for c in range(2):
            pick = (row == h * HEAD + c * HALF + col % HALF).astype(BF16)
            spread.append(
                [
                    jnp.dot(ref[:, 2 * HEAD :], pick, preferred_element_type=F32).astype(BF16)
                    for ref in (before_ref, own_ref)
                ]
            )
        totals = [jnp.zeros((rows, GROUPS * HALF), F32) for _ in range(2)]
        for g in range(GROUPS):
            head = h * GROUPS + g
            q = q_ref[:, head * HEAD : (head + 1) * HEAD]
            s_before = lax.dot_general(q, k_before, contract, preferred_element_type=F32)
            s_own = lax.dot_general(q, k_own, contract, preferred_element_type=F32)
            s_before = jnp.where(allowed_before, s_before * HEAD**-0.5, NEGATIVE)
            s_own = jnp.where(allowed_own, s_own * HEAD**-0.5, NEGATIVE)
            sink = sink_ref[head]
            top = jnp.max(jnp.maximum(s_before, s_own), axis=1, keepdims=True)
            top = jnp.maximum(top, sink)
            e_before = jnp.exp(s_before - top)
            e_own = jnp.exp(s_own - top)
            total = jnp.sum(e_before + e_own, axis=1, keepdims=True) + jnp.exp(sink - top)
            p_before = (e_before / total).astype(BF16)
            p_own = (e_own / total).astype(BF16)
            for c in range(2):
                v_before, v_own = spread[c]
                zero = jnp.zeros_like(v_own)
                mine = group_of_lane == g
                totals[c] += jnp.dot(
                    p_before, jnp.where(mine, v_before, zero), preferred_element_type=F32
                ) + jnp.dot(p_own, jnp.where(mine, v_own, zero), preferred_element_type=F32)
        for c in range(2):
            made = totals[c].astype(BF16)
            for t in range(TP):
                out_ref[t, h, c] = made


def projection_kernel(heads_ref, w_ref, residual_ref, gain_ref, stream_ref, rows_ref):
    stream = residual_ref[...].astype(F32)
    depth = GROUPS * HALF
    for n in range(heads_ref.shape[0]):
        stream += jnp.dot(
            heads_ref[n], w_ref[n * depth : (n + 1) * depth, :], preferred_element_type=F32
        )
    stream_ref[...] = stream
    squares = jnp.sum(stream * stream, axis=1, keepdims=True)
    scaled = (stream * gain_ref[...]).astype(BF16)
    lane = lax.broadcasted_iota(jnp.int32, (stream.shape[0], PADDED - QUARTER), 1)
    high = squares.astype(BF16).astype(F32)
    middle = (squares - high).astype(BF16).astype(F32)
    low = squares - high - middle
    extra = jnp.where(lane == 0, high, jnp.where(lane == 1, middle, jnp.where(lane == 2, low, 0.0)))
    extra = extra.astype(BF16)
    for t in range(TP):
        rows_ref[t, :, :QUARTER] = scaled
        rows_ref[t, :, QUARTER:] = extra


def dispatch_kernel(order_ref, rows_ref, routing_ref, out_ref, flat):
    squares = jnp.zeros((rows_ref.shape[1], 1), F32)
    for t in range(TP):
        squares += jnp.sum(rows_ref[t, :, QUARTER:].astype(F32), axis=1, keepdims=True)
    scale = lax.rsqrt(squares / D + EPSILON)
    routing = routing_ref[...]
    for t in range(TP):
        normed = (rows_ref[order_ref[t]].astype(F32) * scale).astype(BF16)
        picked = jnp.dot(routing, normed, preferred_element_type=F32)
        for b in range(6):
            flat[pl.ds(t * 6 + b, SLOTS, stride=BLOCKS), :] = picked[:, b * 128 : (b + 1) * 128]
    out_ref[...] = flat[...].astype(BF16)


def pack_kernel(gate_ref, up_ref, down_ref, out_ref):
    for n, ref in enumerate((gate_ref, up_ref, down_ref)):
        out_ref[n * QUARTER : (n + 1) * QUARTER, :QUARTER] = ref[...]
    pad = jnp.zeros((out_ref.shape[0], PADDED - QUARTER), BF16)
    out_ref[:, QUARTER:] = pad


def expert_kernel(
    mine_ref,
    other_ref,
    own_ref,
    left_ref,
    right_ref,
    far_a_ref,
    far_b_ref,
    to_mine_ref,
    to_other_ref,
    flat,
    rows,
):
    for n, ref in enumerate((mine_ref, other_ref)):
        flat[...] = ref[...].astype(F32)
        for b in range(BLOCKS):
            lanes = slice(b % 6 * 128, b % 6 * 128 + 128)
            rows[b // 6, n * SLOTS : (n + 1) * SLOTS, lanes] = flat[
                pl.ds(b, SLOTS, stride=BLOCKS), :
            ].astype(BF16)
    gate = jnp.zeros((2 * SLOTS, QUARTER), F32)
    up = jnp.zeros((2 * SLOTS, QUARTER), F32)
    near = (own_ref, left_ref, right_ref)
    for n, ref in enumerate(near):
        part = rows[n, :, :QUARTER]
        gate += jnp.dot(part, ref[:QUARTER, :QUARTER], preferred_element_type=F32)
        up += jnp.dot(part, ref[QUARTER : 2 * QUARTER, :QUARTER], preferred_element_type=F32)
    split = FAR - QUARTER
    gate += jnp.dot(rows[3, :, :QUARTER], far_a_ref[:QUARTER, :QUARTER], preferred_element_type=F32)
    up += jnp.dot(rows[3, :, :split], far_a_ref[QUARTER:, :QUARTER], preferred_element_type=F32)
    up += jnp.dot(
        rows[3, :, split:QUARTER], far_b_ref[: QUARTER - split, :QUARTER], preferred_element_type=F32
    )
    active = (gate / (1.0 + jnp.exp(-gate)) * up).astype(BF16)
    down = [ref[2 * QUARTER :, :] for ref in near] + [far_b_ref[QUARTER - split :, :]]
    for n, ref in enumerate((to_mine_ref, to_other_ref)):
        part = active[n * SLOTS : (n + 1) * SLOTS]
        for t in range(TP):
            made = jnp.dot(part, down[t], preferred_element_type=F32)
            for b in range(6):
                flat[pl.ds(t * 6 + b, SLOTS, stride=BLOCKS), :] = made[:, b * 128 : (b + 1) * 128]
        ref[...] = flat[...].astype(BF16)


def combine_kernel(order_ref, back_ref, mixing_ref, out_ref, flat):
    flat[...] = back_ref[...].astype(F32)
    mixing = mixing_ref[...]
    for t in range(TP):
        for b in range(6):
            part = flat[pl.ds(t * 6 + b, SLOTS, stride=BLOCKS), :].astype(BF16)
            out_ref[order_ref[t], :, b * 128 : (b + 1) * 128] = jnp.dot(
                mixing, part, preferred_element_type=F32
            ).astype(BF16)


def shards(
    queries,
    keys,
    values,
    sinks,
    session_start,
    residual,
    w_out,
    norm_gain,
    expert_ids,
    expert_gates,
    w_gate,
    w_up,
    w_down,
):
    count = queries.shape[0]
    tp = lax.axis_index("tp")
    seq_index = lax.axis_index(SEQ)
    seq_size = lax.axis_size("y") * lax.axis_size("z") * lax.axis_size("core")
    z_size = lax.axis_size("z")
    order = jnp.stack([tp, (tp + 3) % TP, (tp + 1) % TP, (tp + 2) % TP]).astype(jnp.int32)

    with jax.named_scope("expert_weights"):
        packed = call(
            pack_kernel,
            jax.ShapeDtypeStruct((3 * QUARTER, PADDED), BF16),
            (w_gate, w_up, w_down),
            limit=16,
        )
        packed, w_out, keys = lax.optimization_barrier((packed, w_out, keys))
        left, right = shifted(packed, "tp", 1), shifted(packed, "tp", -1)

    with jax.named_scope("projection_rows"):
        spread = jnp.broadcast_to(w_out[None], (z_size,) + w_out.shape)
        column = lax.all_to_all(spread, "z", 0, 0, tiled=True)
        column = column.reshape(z_size * w_out.shape[0], QUARTER)
        w_all = lax.all_gather(column, GATHERED, axis=0, tiled=True)

    with jax.named_scope("attention"):
        pair = jnp.concatenate([keys, values], axis=1)
        before = lax.ppermute(pair, SEQ, [(i, i + 1) for i in range(seq_size - 1)])
        start = (session_start - seq_index * count + WINDOW)[:, None]
        heads = call(
            attention_kernel,
            jax.ShapeDtypeStruct((TP, 2, 2, count, GROUPS * HALF), BF16),
            (queries, pair, before, start, sinks),
            spaces=[pltpu.VMEM] * 4 + [pltpu.SMEM],
            flops=2_000_000_000,
            moved=2_000_000,
            limit=24,
        )
        heads = lax.all_to_all(heads, "tp", 0, 0, tiled=True)
        heads = heads.reshape(TP * 4, count, GROUPS * HALF)

    with jax.named_scope("stream"):
        stream, scaled = call(
            projection_kernel,
            [
                jax.ShapeDtypeStruct((count, QUARTER), F32),
                jax.ShapeDtypeStruct((TP, count, PADDED), BF16),
            ],
            (heads, w_all, residual, norm_gain[None, :]),
            flops=800_000_000,
            moved=8_000_000,
            limit=24,
        )
        scaled = lax.all_to_all(scaled, "tp", 0, 0, tiled=True)
        scaled, left, right = lax.optimization_barrier((scaled, left, right))

    with jax.named_scope("expert_weights"):
        far_a = shifted(left[:FAR], "tp", 1)
        far_b = shifted(right[FAR:], "tp", -1)

    with jax.named_scope("routing"):
        present = expert_ids[:, :, None] == jnp.arange(EXPERTS, dtype=jnp.int32)[None, None, :]
        per_row = jnp.sum(present.astype(jnp.int32), axis=1)
        earlier = jnp.cumsum(per_row, axis=0) - per_row
        position = jnp.sum(jnp.where(present, earlier[:, None, :], 0), axis=2)
        target = jnp.where(
            position % TP == tp, expert_ids * CLASS_SLOTS + position // TP, -1
        )
        slots = jnp.arange(SLOTS, dtype=jnp.int32)
        routing = jnp.sum((slots[:, None, None] == target[None]).astype(BF16), axis=2)
        mixing = jnp.sum(
            jnp.where(
                slots[None, :, None] == target[:, None, :],
                expert_gates[:, None, :],
                jnp.zeros((), BF16),
            ),
            axis=2,
        )

    flat_scratch = pltpu.VMEM((SLOTS * BLOCKS, 128), F32)
    block = (EXPERTS, CLASS_SLOTS * BLOCKS, 128)
    flat_shape = jax.ShapeDtypeStruct((SLOTS * BLOCKS, 128), BF16)
    with jax.named_scope("dispatch"):
        sending = call(dispatch_kernel, flat_shape, (order, scaled, routing), scratch=[flat_scratch], spaces=[pltpu.SMEM] + [pltpu.VMEM] * 2, limit=16)
        arrived = lax.all_to_all(sending.reshape(block), CHIPS, 0, 0, tiled=True)
        partner = shifted(arrived, "core", 1)

    with jax.named_scope("experts"):
        to_mine, to_other = call(
            expert_kernel,
            [flat_shape] * 2,
            (
                arrived.reshape(flat_shape.shape),
                partner.reshape(flat_shape.shape),
                packed,
                left,
                right,
                far_a,
                far_b,
            ),
            scratch=[flat_scratch, pltpu.VMEM((TP, 2 * SLOTS, PADDED), BF16)],
            flops=5_000_000_000,
            moved=15_000_000,
            limit=40,
        )
        received = shifted(to_other, "core", 1)
        both = (to_mine.astype(F32) + received.astype(F32)).astype(BF16)

    with jax.named_scope("combine"):
        back = lax.all_to_all(both.reshape(block), CHIPS, 0, 0, tiled=True)
        mixed = call(
            combine_kernel,
            jax.ShapeDtypeStruct((TP, count, PADDED), BF16),
            (order, back.reshape(flat_shape.shape), mixing),
            scratch=[flat_scratch],
            spaces=[pltpu.SMEM] + [pltpu.VMEM] * 2,
            limit=16,
        )
        mixed = lax.all_to_all(mixed, "tp", 0, 0, tiled=True)
        moe = jnp.sum(mixed[:, :, :QUARTER].astype(F32), axis=0)
        return (stream + moe).astype(BF16)


def solution(mesh):
    whole = Mesh(mesh.devices.reshape(8, 8, 2, 4), ("y", "z", "core", "tp"))
    return jax.shard_map(
        shards,
        mesh=whole,
        in_specs=(
            P(SEQ, "tp"),
            P(SEQ, "tp"),
            P(SEQ, "tp"),
            P("tp"),
            P(SEQ),
            P(SEQ, "tp"),
            P(SEQ, "tp"),
            P("tp"),
            P(SEQ, None),
            P(SEQ, None),
            P("tp", SEQ),
            P("tp", SEQ),
            P(SEQ, "tp"),
        ),
        out_specs=P(SEQ, "tp"),
        check_vma=False,
    )
```

```python
import jax
import jax.numpy as jnp
from jax import lax
from jax.experimental import pallas as pl
from jax.experimental.pallas import tpu as pltpu
from jax.sharding import Mesh, PartitionSpec as P

D = 2880
HEAD = 64
HALF = 32
GROUPS = 8
WINDOW = 128
EXPERTS = 64
TP = 4
QUARTER = 720
PADDED = 768
BLOCKS = 24
CLASS_SLOTS = 3
SLOTS = EXPERTS * CLASS_SLOTS
EPSILON = 1e-05
NEGATIVE = -1e30
F32 = jnp.float32
BF16 = jnp.bfloat16
SEQ = ("y", "z", "core")
CHIPS = ("y", "z")


def shifted(block, axis, distance):
    size = lax.axis_size(axis)
    return lax.ppermute(block, axis, [(i, (i + distance) % size) for i in range(size)])


def call(kernel, out_shape, args, scratch=(), spaces=None, flops=0, moved=0, limit=32, made=pltpu.VMEM):
    spaces = spaces or [pltpu.VMEM] * len(args)
    return pl.pallas_call(
        kernel,
        out_shape=out_shape,
        in_specs=[pl.BlockSpec(memory_space=s) for s in spaces],
        out_specs=jax.tree.map(lambda _: pl.BlockSpec(memory_space=made), out_shape),
        scratch_shapes=list(scratch),
        cost_estimate=pl.CostEstimate(flops=flops, bytes_accessed=moved, transcendentals=0),
        compiler_params=pltpu.CompilerParams(vmem_limit_bytes=limit * 1024 * 1024),
    )(*args)


def attention_kernel(q_ref, own_ref, before_ref, start_ref, sink_ref, out_ref):
    rows = q_ref.shape[0]
    i = lax.broadcasted_iota(jnp.int32, (rows, rows), 0)
    j = lax.broadcasted_iota(jnp.int32, (rows, rows), 1)
    start = start_ref[...]
    allowed_before = (j > i) & (j >= start)
    allowed_own = (j <= i) & (j + WINDOW >= start)
    row = lax.broadcasted_iota(jnp.int32, (2 * HEAD, GROUPS * HALF), 0)
    col = lax.broadcasted_iota(jnp.int32, (2 * HEAD, GROUPS * HALF), 1)
    group_of_lane = lax.broadcasted_iota(jnp.int32, (rows, GROUPS * HALF), 1) // HALF
    contract = (((1,), (1,)), ((), ()))
    for h in range(2):
        lanes = slice(h * HEAD, (h + 1) * HEAD)
        k_own, k_before = own_ref[:, lanes], before_ref[:, lanes]
        spread = []
        for c in range(2):
            pick = (row == h * HEAD + c * HALF + col % HALF).astype(BF16)
            spread.append(
                [
                    jnp.dot(ref[:, 2 * HEAD :], pick, preferred_element_type=F32).astype(BF16)
                    for ref in (before_ref, own_ref)
                ]
            )
        totals = [jnp.zeros((rows, GROUPS * HALF), F32) for _ in range(2)]
        for g in range(GROUPS):
            head = h * GROUPS + g
            q = q_ref[:, head * HEAD : (head + 1) * HEAD]
            s_before = lax.dot_general(q, k_before, contract, preferred_element_type=F32)
            s_own = lax.dot_general(q, k_own, contract, preferred_element_type=F32)
            s_before = jnp.where(allowed_before, s_before * HEAD**-0.5, NEGATIVE)
            s_own = jnp.where(allowed_own, s_own * HEAD**-0.5, NEGATIVE)
            sink = sink_ref[head]
            top = jnp.max(jnp.maximum(s_before, s_own), axis=1, keepdims=True)
            top = jnp.maximum(top, sink)
            e_before = jnp.exp(s_before - top)
            e_own = jnp.exp(s_own - top)
            total = jnp.sum(e_before + e_own, axis=1, keepdims=True) + jnp.exp(sink - top)
            p_before = (e_before / total).astype(BF16)
            p_own = (e_own / total).astype(BF16)
            for c in range(2):
                v_before, v_own = spread[c]
                zero = jnp.zeros_like(v_own)
                mine = group_of_lane == g
                totals[c] += jnp.dot(
                    p_before, jnp.where(mine, v_before, zero), preferred_element_type=F32
                ) + jnp.dot(p_own, jnp.where(mine, v_own, zero), preferred_element_type=F32)
        for c in range(2):
            made = totals[c].astype(BF16)
            for t in range(TP):
                out_ref[c, t, h] = made


def projection_kernel(index_ref, heads_ref, *refs):
    shards, (own_ref, other_ref, total) = refs[:9], refs[9:]
    me = index_ref[8]
    rows = own_ref.shape[0]
    for half in range(2):
        acc = jnp.zeros((rows, QUARTER), F32)
        for n in range(7):
            chunk = heads_ref[half, index_ref[n]]
            acc += jnp.dot(chunk, shards[n][...], preferred_element_type=F32)
        chunk = heads_ref[half, index_ref[7]]
        depth = chunk.shape[1] // 2
        acc += jnp.dot(chunk[:, :depth], shards[7][...], preferred_element_type=F32)
        acc += jnp.dot(chunk[:, depth:], shards[8][...], preferred_element_type=F32)
        total[half] = acc
    own_ref[...] = total[me]
    other_ref[...] = total[1 - me]


def stream_kernel(residual_ref, own_ref, got_ref, gain_ref, stream_ref, rows_ref):
    stream = residual_ref[...].astype(F32) + (own_ref[...] + got_ref[...])
    stream_ref[...] = stream
    squares = jnp.sum(stream * stream, axis=1, keepdims=True)
    scaled = (stream * gain_ref[...]).astype(BF16)
    lane = lax.broadcasted_iota(jnp.int32, (stream.shape[0], PADDED - QUARTER), 1)
    high = squares.astype(BF16).astype(F32)
    middle = (squares - high).astype(BF16).astype(F32)
    low = squares - high - middle
    extra = jnp.where(lane == 0, high, jnp.where(lane == 1, middle, jnp.where(lane == 2, low, 0.0)))
    extra = extra.astype(BF16)
    for t in range(TP):
        rows_ref[t, :, :QUARTER] = scaled
        rows_ref[t, :, QUARTER:] = extra


def dispatch_kernel(order_ref, rows_ref, routing_ref, out_ref, flat):
    squares = jnp.zeros((rows_ref.shape[1], 1), F32)
    for t in range(TP):
        squares += jnp.sum(rows_ref[t, :, QUARTER:].astype(F32), axis=1, keepdims=True)
    scale = lax.rsqrt(squares / D + EPSILON)
    routing = routing_ref[...]
    for t in range(TP):
        normed = (rows_ref[order_ref[t]].astype(F32) * scale).astype(BF16)
        picked = jnp.dot(routing, normed, preferred_element_type=F32)
        for b in range(6):
            flat[pl.ds(t * 6 + b, SLOTS, stride=BLOCKS), :] = picked[:, b * 128 : (b + 1) * 128]
    out_ref[...] = flat[...].astype(BF16)


def pack_kernel(gate_ref, up_ref, out_ref, held, in_sems, out_sems):
    span = QUARTER // 3
    arriving, leaving = [], []
    for n, ref in enumerate((gate_ref, up_ref)):
        for k in range(3):
            rows = pl.ds(k * span, span)
            arriving.append(
                pltpu.make_async_copy(ref.at[rows], held.at[n, rows], in_sems.at[3 * n + k])
            )
            leaving.append(
                pltpu.make_async_copy(
                    held.at[n, rows], out_ref.at[n, rows], out_sems.at[3 * n + k]
                )
            )
    for copy in arriving:
        copy.start()
    for before, after in zip(arriving, leaving):
        before.wait()
        after.start()
    for copy in leaving:
        copy.wait()


def expert_kernel(order_ref, mine_ref, other_ref, *refs):
    sources, (to_mine_ref, to_other_ref, flat, rows, w, sems) = refs[:6], refs[6:]
    half = QUARTER // 2
    copies = []
    for n in range(2):
        for k in range(TP):
            copies.append((sources[0].at[order_ref[k], n], w.at[n * TP + k]))
    for k in range(3):
        copies.append((sources[1 + k], w.at[2 * TP + k]))
    copies.append((sources[4], w.at[2 * TP + 3, pl.ds(0, half)]))
    copies.append((sources[5], w.at[2 * TP + 3, pl.ds(half, half)]))
    copies = [
        pltpu.make_async_copy(src, dst, sems.at[n]) for n, (src, dst) in enumerate(copies)
    ]
    for copy in copies:
        copy.start()
    for n, ref in enumerate((mine_ref, other_ref)):
        flat[...] = ref[...].astype(F32)
        for b in range(BLOCKS):
            lanes = slice(b % 6 * 128, b % 6 * 128 + 128)
            rows[b // 6, n * SLOTS : (n + 1) * SLOTS, lanes] = flat[
                pl.ds(b, SLOTS, stride=BLOCKS), :
            ].astype(BF16)
    sums = []
    for n in range(2):
        total = jnp.zeros((2 * SLOTS, QUARTER), F32)
        for t in range(TP):
            copies[TP * n + t].wait()
            total += jnp.dot(rows[t, :, :QUARTER], w[n * TP + t], preferred_element_type=F32)
        sums.append(total)
    gate, up = sums
    active = (gate / (1.0 + jnp.exp(-gate)) * up).astype(BF16)
    for copy in copies[2 * TP :]:
        copy.wait()
    for n, ref in enumerate((to_mine_ref, to_other_ref)):
        part = active[n * SLOTS : (n + 1) * SLOTS]
        for t in range(TP):
            made = jnp.dot(part, w[2 * TP + t], preferred_element_type=F32)
            made = jnp.concatenate([made, jnp.zeros((SLOTS, PADDED - QUARTER), F32)], axis=1)
            for b in range(6):
                flat[pl.ds(t * 6 + b, SLOTS, stride=BLOCKS), :] = made[:, b * 128 : (b + 1) * 128]
        ref[...] = flat[...].astype(BF16)


def combine_kernel(order_ref, back_ref, mixing_ref, out_ref, flat):
    flat[...] = back_ref[...].astype(F32)
    mixing = mixing_ref[...]
    for t in range(TP):
        for b in range(6):
            part = flat[pl.ds(t * 6 + b, SLOTS, stride=BLOCKS), :].astype(BF16)
            out_ref[order_ref[t], :, b * 128 : (b + 1) * 128] = jnp.dot(
                mixing, part, preferred_element_type=F32
            ).astype(BF16)


def shards(
    queries,
    keys,
    values,
    sinks,
    session_start,
    residual,
    w_out,
    norm_gain,
    expert_ids,
    expert_gates,
    w_gate,
    w_up,
    w_down,
):
    count = queries.shape[0]
    y, core, tp = lax.axis_index("y"), lax.axis_index("core"), lax.axis_index("tp")
    seq_index = lax.axis_index(SEQ)
    seq_size = lax.axis_size("y") * lax.axis_size("z") * lax.axis_size("core")
    y_size, z_size = lax.axis_size("y"), lax.axis_size("z")

    order = jnp.stack([tp, (tp + 3) % TP, (tp + 1) % TP, (tp + 2) % TP]).astype(jnp.int32)

    with jax.named_scope("expert_weights"):
        packed = call(
            pack_kernel,
            jax.ShapeDtypeStruct((2, QUARTER, QUARTER), BF16),
            (w_gate, w_up),
            scratch=[
                pltpu.VMEM((2, QUARTER, QUARTER), BF16),
                pltpu.SemaphoreType.DMA((6,)),
                pltpu.SemaphoreType.DMA((6,)),
            ],
            spaces=[pltpu.HBM] * 2,
            made=pltpu.HBM,
            limit=60,
        )
        gate_up = lax.all_gather(packed, "tp", axis=0, tiled=False)
        packed, w_out, keys = lax.optimization_barrier((packed, w_out, keys))

    with jax.named_scope("projection_rows"):
        spread = jnp.broadcast_to(w_out[None], (z_size,) + w_out.shape)
        column = lax.all_to_all(spread, "z", 0, 0, tiled=True)
        column = column.reshape(z_size * w_out.shape[0], QUARTER)

    with jax.named_scope("attention"):
        pair = jnp.concatenate([keys, values], axis=1)
        before = lax.ppermute(pair, SEQ, [(i, i + 1) for i in range(seq_size - 1)])
        start = (session_start - seq_index * count + WINDOW)[:, None]
        heads = call(
            attention_kernel,
            jax.ShapeDtypeStruct((2, TP, 2, count, GROUPS * HALF), BF16),
            (queries, pair, before, start, sinks),
            spaces=[pltpu.VMEM] * 4 + [pltpu.SMEM],
            flops=2_000_000_000,
            moved=2_000_000,
            limit=24,
        )
        column, heads = lax.optimization_barrier((column, heads))

    with jax.named_scope("projection_rows"):
        half = column.shape[0] // 2
        ahead, behind, pieces = column, column, [column]
        for _ in range(y_size // 2 - 1):
            ahead, behind = shifted(ahead, "y", 1), shifted(behind, "y", -1)
            pieces += [ahead, behind]
        pieces += [shifted(ahead[:half], "y", 1), shifted(behind[half:], "y", -1)]
        sources = [y]
        for k in range(1, y_size // 2):
            sources += [(y - k) % y_size, (y + k) % y_size]
        sources.append((y + y_size // 2) % y_size)
        index = jnp.stack([jnp.asarray(v, jnp.int32) for v in sources + [core]])

    with jax.named_scope("attention"):
        heads = lax.all_to_all(
            heads.reshape(2 * TP, 2, count, GROUPS * HALF), ("core", "tp"), 0, 0, tiled=True
        )
        heads = heads.reshape(2, TP * 2, count, GROUPS * HALF)

    with jax.named_scope("stream"):
        own, other = call(
            projection_kernel,
            [jax.ShapeDtypeStruct((count, QUARTER), F32)] * 2,
            (index, heads, *pieces),
            scratch=[pltpu.VMEM((2, count, QUARTER), F32)],
            spaces=[pltpu.SMEM] + [pltpu.VMEM] * 10,
            flops=800_000_000,
            moved=4_000_000,
        )
        got = shifted(other, "core", 1)
        stream, scaled = call(
            stream_kernel,
            [
                jax.ShapeDtypeStruct((count, QUARTER), F32),
                jax.ShapeDtypeStruct((TP, count, PADDED), BF16),
            ],
            (residual, own, got, norm_gain[None, :]),
        )
        scaled = lax.all_to_all(scaled, "tp", 0, 0, tiled=True)
        scaled, w_down = lax.optimization_barrier((scaled, w_down))

    with jax.named_scope("expert_weights"):
        left, right = shifted(w_down, "tp", 1), shifted(w_down, "tp", -1)
        part = QUARTER // 2
        far = [shifted(left[:part], "tp", 1), shifted(right[part:], "tp", -1)]

    with jax.named_scope("routing"):
        present = expert_ids[:, :, None] == jnp.arange(EXPERTS, dtype=jnp.int32)[None, None, :]
        per_row = jnp.sum(present.astype(jnp.int32), axis=1)
        earlier = jnp.cumsum(per_row, axis=0) - per_row
        position = jnp.sum(jnp.where(present, earlier[:, None, :], 0), axis=2)
        target = jnp.where(
            position % TP == tp, expert_ids * CLASS_SLOTS + position // TP, -1
        )
        slots = jnp.arange(SLOTS, dtype=jnp.int32)
        routing = jnp.sum((slots[:, None, None] == target[None]).astype(BF16), axis=2)
        mixing = jnp.sum(
            jnp.where(
                slots[None, :, None] == target[:, None, :],
                expert_gates[:, None, :],
                jnp.zeros((), BF16),
            ),
            axis=2,
        )

    flat_scratch = pltpu.VMEM((SLOTS * BLOCKS, 128), F32)
    block = (EXPERTS, CLASS_SLOTS * BLOCKS, 128)
    flat_shape = jax.ShapeDtypeStruct((SLOTS * BLOCKS, 128), BF16)
    with jax.named_scope("dispatch"):
        sending = call(dispatch_kernel, flat_shape, (order, scaled, routing), scratch=[flat_scratch], spaces=[pltpu.SMEM] + [pltpu.VMEM] * 2, limit=16)
        arrived = lax.all_to_all(sending.reshape(block), CHIPS, 0, 0, tiled=True)
        arrived, left, right, far = lax.optimization_barrier((arrived, left, right, far))
        partner = shifted(arrived, "core", 1)

    with jax.named_scope("experts"):
        to_mine, to_other = call(
            expert_kernel,
            [flat_shape] * 2,
            (
                order,
                arrived.reshape(flat_shape.shape),
                partner.reshape(flat_shape.shape),
                gate_up,
                w_down,
                left,
                right,
                *far,
            ),
            scratch=[
                flat_scratch,
                pltpu.VMEM((TP, 2 * SLOTS, PADDED), BF16),
                pltpu.VMEM((3 * TP, QUARTER, QUARTER), BF16),
                pltpu.SemaphoreType.DMA((13,)),
            ],
            spaces=[pltpu.SMEM] + [pltpu.VMEM] * 2 + [pltpu.HBM] * 6,
            flops=5_000_000_000,
            moved=15_000_000,
            limit=58,
        )
        received = shifted(to_other, "core", 1)
        both = (to_mine.astype(F32) + received.astype(F32)).astype(BF16)

    with jax.named_scope("combine"):
        back = lax.all_to_all(both.reshape(block), CHIPS, 0, 0, tiled=True)
        mixed = call(
            combine_kernel,
            jax.ShapeDtypeStruct((TP, count, PADDED), BF16),
            (order, back.reshape(flat_shape.shape), mixing),
            scratch=[flat_scratch],
            spaces=[pltpu.SMEM] + [pltpu.VMEM] * 2,
            limit=16,
        )
        mixed = lax.all_to_all(mixed, "tp", 0, 0, tiled=True)
        moe = jnp.sum(mixed[:, :, :QUARTER].astype(F32), axis=0)
        return (stream + moe).astype(BF16)


def solution(mesh):
    whole = Mesh(mesh.devices.reshape(8, 8, 2, 4), ("y", "z", "core", "tp"))
    return jax.shard_map(
        shards,
        mesh=whole,
        in_specs=(
            P(SEQ, "tp"),
            P(SEQ, "tp"),
            P(SEQ, "tp"),
            P("tp"),
            P(SEQ),
            P(SEQ, "tp"),
            P(SEQ, "tp"),
            P("tp"),
            P(SEQ, None),
            P(SEQ, None),
            P("tp", SEQ),
            P("tp", SEQ),
            P(SEQ, "tp"),
        ),
        out_specs=P(SEQ, "tp"),
        check_vma=False,
    )
```

```python
import jax
import jax.numpy as jnp
from jax import lax
from jax.experimental import pallas as pl
from jax.experimental.pallas import tpu as pltpu
from jax.sharding import Mesh, PartitionSpec as P

D = 2880
HEAD = 64
HALF = 32
GROUPS = 8
WINDOW = 128
EXPERTS = 64
TP = 4
QUARTER = 720
PADDED = 768
CHUNK = 18
TARGETS = EXPERTS * TP
CLASS_SLOTS = 3
SLOTS = EXPERTS * CLASS_SLOTS
EPSILON = 1e-05
NEGATIVE = -1e30
F32 = jnp.float32
BF16 = jnp.bfloat16
SEQ = ("y", "z", "core")
PLANE = ("y", "z", "tp")


def shifted(block, axis, distance):
    size = lax.axis_size(axis)
    return lax.ppermute(block, axis, [(i, (i + distance) % size) for i in range(size)])


def call(kernel, out_shape, args, scratch=(), spaces=None, flops=0, moved=0, limit=32, made=pltpu.VMEM):
    spaces = spaces or [pltpu.VMEM] * len(args)
    return pl.pallas_call(
        kernel,
        out_shape=out_shape,
        in_specs=[pl.BlockSpec(memory_space=s) for s in spaces],
        out_specs=jax.tree.map(lambda _: pl.BlockSpec(memory_space=made), out_shape),
        scratch_shapes=list(scratch),
        cost_estimate=pl.CostEstimate(flops=flops, bytes_accessed=moved, transcendentals=0),
        compiler_params=pltpu.CompilerParams(vmem_limit_bytes=limit * 1024 * 1024),
    )(*args)


def attention_kernel(q_ref, own_ref, before_ref, start_ref, sink_ref, out_ref):
    rows = q_ref.shape[0]
    i = lax.broadcasted_iota(jnp.int32, (rows, rows), 0)
    j = lax.broadcasted_iota(jnp.int32, (rows, rows), 1)
    start = start_ref[...]
    allowed_before = (j > i) & (j >= start)
    allowed_own = (j <= i) & (j + WINDOW >= start)
    row = lax.broadcasted_iota(jnp.int32, (2 * HEAD, GROUPS * HALF), 0)
    col = lax.broadcasted_iota(jnp.int32, (2 * HEAD, GROUPS * HALF), 1)
    group_of_lane = lax.broadcasted_iota(jnp.int32, (rows, GROUPS * HALF), 1) // HALF
    contract = (((1,), (1,)), ((), ()))
    for h in range(2):
        lanes = slice(h * HEAD, (h + 1) * HEAD)
        k_own, k_before = own_ref[:, lanes], before_ref[:, lanes]
        spread = []
        for c in range(2):
            pick = (row == h * HEAD + c * HALF + col % HALF).astype(BF16)
            spread.append(
                [
                    jnp.dot(ref[:, 2 * HEAD :], pick, preferred_element_type=F32).astype(BF16)
                    for ref in (before_ref, own_ref)
                ]
            )
        totals = [jnp.zeros((rows, GROUPS * HALF), F32) for _ in range(2)]
        for g in range(GROUPS):
            head = h * GROUPS + g
            q = q_ref[:, head * HEAD : (head + 1) * HEAD]
            s_before = lax.dot_general(q, k_before, contract, preferred_element_type=F32)
            s_own = lax.dot_general(q, k_own, contract, preferred_element_type=F32)
            s_before = jnp.where(allowed_before, s_before * HEAD**-0.5, NEGATIVE)
            s_own = jnp.where(allowed_own, s_own * HEAD**-0.5, NEGATIVE)
            sink = sink_ref[head]
            top = jnp.max(jnp.maximum(s_before, s_own), axis=1, keepdims=True)
            top = jnp.maximum(top, sink)
            e_before = jnp.exp(s_before - top)
            e_own = jnp.exp(s_own - top)
            total = jnp.sum(e_before + e_own, axis=1, keepdims=True) + jnp.exp(sink - top)
            p_before = (e_before / total).astype(BF16)
            p_own = (e_own / total).astype(BF16)
            for c in range(2):
                v_before, v_own = spread[c]
                zero = jnp.zeros_like(v_own)
                mine = group_of_lane == g
                totals[c] += jnp.dot(
                    p_before, jnp.where(mine, v_before, zero), preferred_element_type=F32
                ) + jnp.dot(p_own, jnp.where(mine, v_own, zero), preferred_element_type=F32)
        for c in range(2):
            made = totals[c].astype(BF16)
            for t in range(TP):
                out_ref[c, t, h] = made


def projection_kernel(index_ref, heads_ref, *refs):
    shards, (own_ref, other_ref, total) = refs[:9], refs[9:]
    me = index_ref[8]
    rows = own_ref.shape[0]
    for half in range(2):
        acc = jnp.zeros((rows, QUARTER), F32)
        for n in range(7):
            chunk = heads_ref[half, index_ref[n]]
            acc += jnp.dot(chunk, shards[n][...], preferred_element_type=F32)
        chunk = heads_ref[half, index_ref[7]]
        depth = chunk.shape[1] // 2
        acc += jnp.dot(chunk[:, :depth], shards[7][...], preferred_element_type=F32)
        acc += jnp.dot(chunk[:, depth:], shards[8][...], preferred_element_type=F32)
        total[half] = acc
    own_ref[...] = total[me]
    other_ref[...] = total[1 - me]


def stream_kernel(residual_ref, own_ref, got_ref, gain_ref, stream_ref, rows_ref):
    stream = residual_ref[...].astype(F32) + (own_ref[...] + got_ref[...])
    stream_ref[...] = stream
    squares = jnp.sum(stream * stream, axis=1, keepdims=True)
    scaled = (stream * gain_ref[...]).astype(BF16)
    lane = lax.broadcasted_iota(jnp.int32, (stream.shape[0], PADDED - QUARTER), 1)
    high = squares.astype(BF16).astype(F32)
    middle = (squares - high).astype(BF16).astype(F32)
    low = squares - high - middle
    extra = jnp.where(lane == 0, high, jnp.where(lane == 1, middle, jnp.where(lane == 2, low, 0.0)))
    extra = extra.astype(BF16)
    rows_ref[:, :QUARTER] = scaled
    rows_ref[:, QUARTER:] = extra


def dispatch_kernel(rows_ref, routing_ref, out_ref, flat):
    picked = jnp.dot(routing_ref[...], rows_ref[...], preferred_element_type=F32)
    for k in range(CLASS_SLOTS):
        for b in range(6):
            flat[pl.ds(k * 6 + b, TARGETS, stride=CHUNK), :] = picked[
                k * TARGETS : (k + 1) * TARGETS, b * 128 : (b + 1) * 128
            ]
    out_ref[...] = flat[...].astype(BF16)


def pack_kernel(gate_ref, up_ref, down_ref, out_ref, held, in_sems, out_sems):
    span = QUARTER // 3
    arriving, leaving = [], []
    for n, ref in enumerate((gate_ref, up_ref, down_ref)):
        for k in range(3):
            rows = pl.ds(k * span, span)
            arriving.append(
                pltpu.make_async_copy(ref.at[rows], held.at[n, rows], in_sems.at[3 * n + k])
            )
            leaving.append(
                pltpu.make_async_copy(
                    held.at[n, rows], out_ref.at[n, rows], out_sems.at[3 * n + k]
                )
            )
    for copy in arriving:
        copy.start()
    for before, after in zip(arriving, leaving):
        before.wait()
        after.start()
    for copy in leaving:
        copy.wait()


def expert_kernel(
    mine_ref, other_ref, weights_ref, to_mine_ref, to_other_ref, flat, rows, w, sems
):
    copies = []
    for n in range(3):
        for t in range(TP):
            copies.append(
                pltpu.make_async_copy(weights_ref.at[t, n], w.at[n * TP + t], sems.at[n * TP + t])
            )
            copies[-1].start()
    squares = []
    for n, ref in enumerate((mine_ref, other_ref)):
        flat[...] = ref[...].astype(F32)
        for k in range(CLASS_SLOTS):
            part = slice(n * SLOTS + k * EXPERTS, n * SLOTS + (k + 1) * EXPERTS)
            total = jnp.zeros((EXPERTS, 1), F32)
            for t in range(TP):
                for b in range(6):
                    piece = flat[pl.ds(t * CHUNK + k * 6 + b, EXPERTS, stride=TP * CHUNK), :]
                    rows[t, part, b * 128 : (b + 1) * 128] = piece.astype(BF16)
                lane = lax.broadcasted_iota(jnp.int32, piece.shape, 1)
                total += jnp.sum(
                    jnp.where(lane >= QUARTER - 5 * 128, piece, 0.0), axis=1, keepdims=True
                )
            squares.append(total)
    scale = lax.rsqrt(jnp.concatenate(squares, axis=0) / D + EPSILON)
    sums = []
    for n in range(2):
        total = jnp.zeros((2 * SLOTS, QUARTER), F32)
        for t in range(TP):
            copies[TP * n + t].wait()
            total += jnp.dot(rows[t, :, :QUARTER], w[n * TP + t], preferred_element_type=F32)
        sums.append(total * scale)
    gate, up = sums
    active = (gate / (1.0 + jnp.exp(-gate)) * up).astype(BF16)
    for copy in copies[2 * TP :]:
        copy.wait()
    for n, ref in enumerate((to_mine_ref, to_other_ref)):
        part = active[n * SLOTS : (n + 1) * SLOTS]
        for t in range(TP):
            made = jnp.dot(part, w[2 * TP + t], preferred_element_type=F32)
            made = jnp.concatenate([made, jnp.zeros((SLOTS, PADDED - QUARTER), F32)], axis=1)
            for k in range(CLASS_SLOTS):
                for b in range(6):
                    flat[pl.ds(t * CHUNK + k * 6 + b, EXPERTS, stride=TP * CHUNK), :] = made[
                        k * EXPERTS : (k + 1) * EXPERTS, b * 128 : (b + 1) * 128
                    ]
        ref[...] = flat[...].astype(BF16)


def combine_kernel(back_ref, mixing_ref, stream_ref, out_ref, flat):
    flat[...] = back_ref[...].astype(F32)
    for b in range(6):
        total = jnp.zeros((out_ref.shape[0], 128), F32)
        for k in range(CLASS_SLOTS):
            part = flat[pl.ds(k * 6 + b, TARGETS, stride=CHUNK), :].astype(BF16)
            total += jnp.dot(
                mixing_ref[:, k * TARGETS : (k + 1) * TARGETS], part, preferred_element_type=F32
            )
        width = min(128, QUARTER - b * 128)
        lanes = slice(b * 128, b * 128 + width)
        out_ref[:, lanes] = (stream_ref[:, lanes] + total[:, :width]).astype(BF16)


def shards(
    queries,
    keys,
    values,
    sinks,
    session_start,
    residual,
    w_out,
    norm_gain,
    expert_ids,
    expert_gates,
    w_gate,
    w_up,
    w_down,
):
    count = queries.shape[0]
    y, core, tp = lax.axis_index("y"), lax.axis_index("core"), lax.axis_index("tp")
    seq_index = lax.axis_index(SEQ)
    seq_size = lax.axis_size("y") * lax.axis_size("z") * lax.axis_size("core")
    y_size, z_size = lax.axis_size("y"), lax.axis_size("z")

    with jax.named_scope("expert_weights"):
        packed = call(
            pack_kernel,
            jax.ShapeDtypeStruct((3, QUARTER, QUARTER), BF16),
            (w_gate, w_up, w_down),
            scratch=[
                pltpu.VMEM((3, QUARTER, QUARTER), BF16),
                pltpu.SemaphoreType.DMA((9,)),
                pltpu.SemaphoreType.DMA((9,)),
            ],
            spaces=[pltpu.HBM] * 3,
            made=pltpu.HBM,
            limit=60,
        )
        weights = lax.all_gather(packed, "tp", axis=0, tiled=False)
        packed, w_out, keys = lax.optimization_barrier((packed, w_out, keys))

    with jax.named_scope("projection_rows"):
        spread = jnp.broadcast_to(w_out[None], (z_size,) + w_out.shape)
        column = lax.all_to_all(spread, "z", 0, 0, tiled=True)
        column = column.reshape(z_size * w_out.shape[0], QUARTER)

    with jax.named_scope("attention"):
        pair = jnp.concatenate([keys, values], axis=1)
        before = lax.ppermute(pair, SEQ, [(i, i + 1) for i in range(seq_size - 1)])
        start = (session_start - seq_index * count + WINDOW)[:, None]
        heads = call(
            attention_kernel,
            jax.ShapeDtypeStruct((2, TP, 2, count, GROUPS * HALF), BF16),
            (queries, pair, before, start, sinks),
            spaces=[pltpu.VMEM] * 4 + [pltpu.SMEM],
            flops=2_000_000_000,
            moved=2_000_000,
            limit=24,
        )
        column, heads = lax.optimization_barrier((column, heads))

    with jax.named_scope("projection_rows"):
        half = column.shape[0] // 2
        ahead, behind, pieces = column, column, [column]
        for _ in range(y_size // 2 - 1):
            ahead, behind = shifted(ahead, "y", 1), shifted(behind, "y", -1)
            pieces += [ahead, behind]
        pieces += [shifted(ahead[:half], "y", 1), shifted(behind[half:], "y", -1)]
        sources = [y]
        for k in range(1, y_size // 2):
            sources += [(y - k) % y_size, (y + k) % y_size]
        sources.append((y + y_size // 2) % y_size)
        index = jnp.stack([jnp.asarray(v, jnp.int32) for v in sources + [core]])

    with jax.named_scope("attention"):
        heads = lax.all_to_all(
            heads.reshape(2 * TP, 2, count, GROUPS * HALF), ("core", "tp"), 0, 0, tiled=True
        )
        heads = heads.reshape(2, TP * 2, count, GROUPS * HALF)

    with jax.named_scope("stream"):
        own, other = call(
            projection_kernel,
            [jax.ShapeDtypeStruct((count, QUARTER), F32)] * 2,
            (index, heads, *pieces),
            scratch=[pltpu.VMEM((2, count, QUARTER), F32)],
            spaces=[pltpu.SMEM] + [pltpu.VMEM] * 10,
            flops=800_000_000,
            moved=4_000_000,
        )
        got = shifted(other, "core", 1)
        stream, scaled = call(
            stream_kernel,
            [
                jax.ShapeDtypeStruct((count, QUARTER), F32),
                jax.ShapeDtypeStruct((count, PADDED), BF16),
            ],
            (residual, own, got, norm_gain[None, :]),
        )

    with jax.named_scope("routing"):
        present = expert_ids[:, :, None] == jnp.arange(EXPERTS, dtype=jnp.int32)[None, None, :]
        per_row = jnp.sum(present.astype(jnp.int32), axis=1)
        earlier = jnp.cumsum(per_row, axis=0) - per_row
        position = jnp.sum(jnp.where(present, earlier[:, None, :], 0), axis=2)
        target = (position // TP) * TARGETS + expert_ids * TP + position % TP
        slots = jnp.arange(CLASS_SLOTS * TARGETS, dtype=jnp.int32)
        routing = jnp.sum((slots[:, None, None] == target[None]).astype(BF16), axis=2)
        mixing = jnp.sum(
            jnp.where(
                slots[None, :, None] == target[:, None, :],
                expert_gates[:, None, :],
                jnp.zeros((), BF16),
            ),
            axis=2,
        )

    flat_scratch = pltpu.VMEM((TARGETS * CHUNK, 128), F32)
    flat_shape = jax.ShapeDtypeStruct((TARGETS * CHUNK, 128), BF16)

    def exchanged(block):
        block = block.reshape(TARGETS, CHUNK // 2, 2, 128)
        return lax.all_to_all(block, PLANE, 0, 0, tiled=True).reshape(flat_shape.shape)

    with jax.named_scope("dispatch"):
        sending = call(
            dispatch_kernel, flat_shape, (scaled, routing), scratch=[flat_scratch], limit=16
        )
        arrived = exchanged(sending)
        partner = shifted(arrived, "core", 1)

    with jax.named_scope("experts"):
        to_mine, to_other = call(
            expert_kernel,
            [flat_shape] * 2,
            (arrived, partner, weights),
            scratch=[
                flat_scratch,
                pltpu.VMEM((TP, 2 * SLOTS, PADDED), BF16),
                pltpu.VMEM((3 * TP, QUARTER, QUARTER), BF16),
                pltpu.SemaphoreType.DMA((3 * TP,)),
            ],
            spaces=[pltpu.VMEM] * 2 + [pltpu.HBM],
            flops=5_000_000_000,
            moved=15_000_000,
            limit=48,
        )
        received = shifted(to_other, "core", 1)
        both = (to_mine.astype(F32) + received.astype(F32)).astype(BF16)

    with jax.named_scope("combine"):
        back = exchanged(both)
        return call(
            combine_kernel,
            jax.ShapeDtypeStruct((count, QUARTER), BF16),
            (back, mixing, stream),
            scratch=[flat_scratch],
            limit=16,
        )


def solution(mesh):
    whole = Mesh(mesh.devices.reshape(8, 8, 2, 4), ("y", "z", "core", "tp"))
    return jax.shard_map(
        shards,
        mesh=whole,
        in_specs=(
            P(SEQ, "tp"),
            P(SEQ, "tp"),
            P(SEQ, "tp"),
            P("tp"),
            P(SEQ),
            P(SEQ, "tp"),
            P(SEQ, "tp"),
            P("tp"),
            P(SEQ, None),
            P(SEQ, None),
            P("tp", SEQ),
            P("tp", SEQ),
            P(SEQ, "tp"),
        ),
        out_specs=P(SEQ, "tp"),
        check_vma=False,
    )
```

```python
import jax
import jax.numpy as jnp
from jax import lax
from jax.experimental import pallas as pl
from jax.experimental.pallas import tpu as pltpu
from jax.sharding import Mesh, PartitionSpec as P

D = 2880
HEAD = 64
HALF = 32
GROUPS = 8
WINDOW = 128
EXPERTS = 64
TP = 4
QUARTER = 720
PADDED = 768
MAIN = 640
TAIL = 80
PACKED = 3 * MAIN + 2 * 128
CHUNK = 18
TARGETS = EXPERTS * TP
CLASS_SLOTS = 3
SLOTS = EXPERTS * CLASS_SLOTS
EPSILON = 1e-05
NEGATIVE = -1e30
F32 = jnp.float32
BF16 = jnp.bfloat16
SEQ = ("y", "z", "core")
PLANE = ("y", "z", "tp")


def shifted(block, axis, distance):
    size = lax.axis_size(axis)
    return lax.ppermute(block, axis, [(i, (i + distance) % size) for i in range(size)])


def call(kernel, out_shape, args, scratch=(), spaces=None, flops=0, moved=0, limit=32, made=pltpu.VMEM):
    spaces = spaces or [pltpu.VMEM] * len(args)
    return pl.pallas_call(
        kernel,
        out_shape=out_shape,
        in_specs=[pl.BlockSpec(memory_space=s) for s in spaces],
        out_specs=jax.tree.map(lambda _: pl.BlockSpec(memory_space=made), out_shape),
        scratch_shapes=list(scratch),
        cost_estimate=pl.CostEstimate(flops=flops, bytes_accessed=moved, transcendentals=0),
        compiler_params=pltpu.CompilerParams(vmem_limit_bytes=limit * 1024 * 1024),
    )(*args)


def attention_kernel(q_ref, own_ref, before_ref, start_ref, sink_ref, out_ref):
    rows = q_ref.shape[0]
    i = lax.broadcasted_iota(jnp.int32, (rows, rows), 0)
    j = lax.broadcasted_iota(jnp.int32, (rows, rows), 1)
    start = start_ref[...]
    allowed_before = (j > i) & (j >= start)
    allowed_own = (j <= i) & (j + WINDOW >= start)
    row = lax.broadcasted_iota(jnp.int32, (2 * HEAD, GROUPS * HALF), 0)
    col = lax.broadcasted_iota(jnp.int32, (2 * HEAD, GROUPS * HALF), 1)
    group_of_lane = lax.broadcasted_iota(jnp.int32, (rows, GROUPS * HALF), 1) // HALF
    contract = (((1,), (1,)), ((), ()))
    for h in range(2):
        lanes = slice(h * HEAD, (h + 1) * HEAD)
        k_own, k_before = own_ref[:, lanes], before_ref[:, lanes]
        spread = []
        for c in range(2):
            pick = (row == h * HEAD + c * HALF + col % HALF).astype(BF16)
            spread.append(
                [
                    jnp.dot(ref[:, 2 * HEAD :], pick, preferred_element_type=F32).astype(BF16)
                    for ref in (before_ref, own_ref)
                ]
            )
        totals = [jnp.zeros((rows, GROUPS * HALF), F32) for _ in range(2)]
        for g in range(GROUPS):
            head = h * GROUPS + g
            q = q_ref[:, head * HEAD : (head + 1) * HEAD]
            s_before = lax.dot_general(q, k_before, contract, preferred_element_type=F32)
            s_own = lax.dot_general(q, k_own, contract, preferred_element_type=F32)
            s_before = jnp.where(allowed_before, s_before * HEAD**-0.5, NEGATIVE)
            s_own = jnp.where(allowed_own, s_own * HEAD**-0.5, NEGATIVE)
            sink = sink_ref[head]
            top = jnp.max(jnp.maximum(s_before, s_own), axis=1, keepdims=True)
            top = jnp.maximum(top, sink)
            e_before = jnp.exp(s_before - top)
            e_own = jnp.exp(s_own - top)
            total = jnp.sum(e_before + e_own, axis=1, keepdims=True) + jnp.exp(sink - top)
            p_before = (e_before / total).astype(BF16)
            p_own = (e_own / total).astype(BF16)
            for c in range(2):
                v_before, v_own = spread[c]
                zero = jnp.zeros_like(v_own)
                mine = group_of_lane == g
                totals[c] += jnp.dot(
                    p_before, jnp.where(mine, v_before, zero), preferred_element_type=F32
                ) + jnp.dot(p_own, jnp.where(mine, v_own, zero), preferred_element_type=F32)
        for c in range(2):
            made = totals[c].astype(BF16)
            for t in range(TP):
                out_ref[c, t, h] = made


def projection_kernel(index_ref, heads_ref, *refs):
    shards, (own_ref, other_ref, total) = refs[:9], refs[9:]
    me = index_ref[8]
    rows = own_ref.shape[0]
    for half in range(2):
        acc = jnp.zeros((rows, QUARTER), F32)
        for n in range(7):
            chunk = heads_ref[half, index_ref[n]]
            acc += jnp.dot(chunk, shards[n][...], preferred_element_type=F32)
        chunk = heads_ref[half, index_ref[7]]
        depth = chunk.shape[1] // 2
        acc += jnp.dot(chunk[:, :depth], shards[7][...], preferred_element_type=F32)
        acc += jnp.dot(chunk[:, depth:], shards[8][...], preferred_element_type=F32)
        total[half] = acc
    own_ref[...] = total[me]
    other_ref[...] = total[1 - me]


def stream_kernel(residual_ref, own_ref, got_ref, gain_ref, stream_ref, rows_ref):
    stream = residual_ref[...].astype(F32) + (own_ref[...] + got_ref[...])
    stream_ref[...] = stream
    squares = jnp.sum(stream * stream, axis=1, keepdims=True)
    scaled = (stream * gain_ref[...]).astype(BF16)
    lane = lax.broadcasted_iota(jnp.int32, (stream.shape[0], PADDED - QUARTER), 1)
    high = squares.astype(BF16).astype(F32)
    middle = (squares - high).astype(BF16).astype(F32)
    low = squares - high - middle
    extra = jnp.where(lane == 0, high, jnp.where(lane == 1, middle, jnp.where(lane == 2, low, 0.0)))
    extra = extra.astype(BF16)
    rows_ref[:, :QUARTER] = scaled
    rows_ref[:, QUARTER:] = extra


def dispatch_kernel(rows_ref, routing_ref, out_ref, flat):
    picked = jnp.dot(routing_ref[...], rows_ref[...], preferred_element_type=F32)
    for k in range(CLASS_SLOTS):
        for b in range(6):
            flat[pl.ds(k * 6 + b, TARGETS, stride=CHUNK), :] = picked[
                k * TARGETS : (k + 1) * TARGETS, b * 128 : (b + 1) * 128
            ]
    out_ref[...] = flat[...].astype(BF16)


def pack_kernel(gate_ref, up_ref, down_ref, out_ref, held, made, in_sems, out_sems):
    refs = (gate_ref, up_ref, down_ref)
    span = QUARTER // 3
    arriving, leaving = [], []
    for k in range(3):
        rows = pl.ds(k * span, span)
        for n, ref in enumerate(refs):
            arriving.append(
                pltpu.make_async_copy(ref.at[rows], held.at[n, rows], in_sems.at[3 * k + n])
            )
            arriving[-1].start()
        leaving.append(pltpu.make_async_copy(made.at[rows], out_ref.at[rows], out_sems.at[k]))
    for k in range(3):
        rows = slice(k * span, (k + 1) * span)
        tails = []
        for n in range(3):
            arriving[3 * k + n].wait()
            made[rows, n * MAIN : (n + 1) * MAIN] = held[n, rows, :MAIN]
            tails.append(held[n, rows, MAIN:])
        tails.append(jnp.zeros((span, 2 * 128 - 3 * TAIL), BF16))
        made[rows, 3 * MAIN :] = jnp.concatenate(tails, axis=1)
        leaving[k].start()
    for copy in leaving:
        copy.wait()


def rows_kernel(mine_ref, other_ref, rows_ref, scale_ref, flat):
    squares = []
    for n, ref in enumerate((mine_ref, other_ref)):
        flat[...] = ref[...].astype(F32)
        for k in range(CLASS_SLOTS):
            part = slice(n * SLOTS + k * EXPERTS, n * SLOTS + (k + 1) * EXPERTS)
            total = jnp.zeros((EXPERTS, 1), F32)
            for t in range(TP):
                for b in range(6):
                    piece = flat[pl.ds(t * CHUNK + k * 6 + b, EXPERTS, stride=TP * CHUNK), :]
                    rows_ref[t, part, b * 128 : (b + 1) * 128] = piece.astype(BF16)
                lane = lax.broadcasted_iota(jnp.int32, piece.shape, 1)
                total += jnp.sum(jnp.where(lane >= TAIL, piece, 0.0), axis=1, keepdims=True)
            squares.append(total)
    scale_ref[...] = lax.rsqrt(jnp.concatenate(squares, axis=0) / D + EPSILON)


def expert_kernel(
    rows_ref, scale_ref, weights_ref, to_mine_ref, to_other_ref, flat, rows, w, sems
):
    copies = []
    for t in range(TP):
        copies.append(
            (
                pltpu.make_async_copy(rows_ref.at[t], rows.at[t], sems.at[2 * t]),
                pltpu.make_async_copy(weights_ref.at[t], w.at[t], sems.at[2 * t + 1]),
            )
        )
        for copy in copies[-1]:
            copy.start()
    sums = jnp.zeros((2 * SLOTS, 2 * MAIN), F32)
    ends = jnp.zeros((2 * SLOTS, 2 * 128), F32)
    for t in range(TP):
        for copy in copies[t]:
            copy.wait()
        part = rows[t, :, :QUARTER]
        sums += jnp.dot(part, w[t, :, : 2 * MAIN], preferred_element_type=F32)
        ends += jnp.dot(part, w[t, :, 3 * MAIN :], preferred_element_type=F32)
    scale = scale_ref[...]
    gate = jnp.concatenate([sums[:, :MAIN], ends[:, :TAIL]], axis=1) * scale
    up = jnp.concatenate([sums[:, MAIN:], ends[:, TAIL : 2 * TAIL]], axis=1) * scale
    active = (gate / (1.0 + jnp.exp(-gate)) * up).astype(BF16)
    for n, ref in enumerate((to_mine_ref, to_other_ref)):
        part = active[n * SLOTS : (n + 1) * SLOTS]
        for t in range(TP):
            made = jnp.dot(part, w[t, :, 2 * MAIN : 3 * MAIN], preferred_element_type=F32)
            last = jnp.dot(part, w[t, :, 3 * MAIN :], preferred_element_type=F32)
            last = jnp.concatenate(
                [last[:, 2 * TAIL : 3 * TAIL], jnp.zeros((SLOTS, 128 - TAIL), F32)], axis=1
            )
            for k in range(CLASS_SLOTS):
                group = slice(k * EXPERTS, (k + 1) * EXPERTS)
                for b in range(6):
                    piece = made[group, b * 128 : (b + 1) * 128] if b < 5 else last[group]
                    flat[pl.ds(t * CHUNK + k * 6 + b, EXPERTS, stride=TP * CHUNK), :] = piece
        ref[...] = flat[...].astype(BF16)


def combine_kernel(back_ref, mixing_ref, stream_ref, out_ref, flat):
    flat[...] = back_ref[...].astype(F32)
    for b in range(6):
        total = jnp.zeros((out_ref.shape[0], 128), F32)
        for k in range(CLASS_SLOTS):
            part = flat[pl.ds(k * 6 + b, TARGETS, stride=CHUNK), :].astype(BF16)
            total += jnp.dot(
                mixing_ref[:, k * TARGETS : (k + 1) * TARGETS], part, preferred_element_type=F32
            )
        width = min(128, QUARTER - b * 128)
        lanes = slice(b * 128, b * 128 + width)
        out_ref[:, lanes] = (stream_ref[:, lanes] + total[:, :width]).astype(BF16)


def shards(
    queries,
    keys,
    values,
    sinks,
    session_start,
    residual,
    w_out,
    norm_gain,
    expert_ids,
    expert_gates,
    w_gate,
    w_up,
    w_down,
):
    count = queries.shape[0]
    y, core, tp = lax.axis_index("y"), lax.axis_index("core"), lax.axis_index("tp")
    seq_index = lax.axis_index(SEQ)
    seq_size = lax.axis_size("y") * lax.axis_size("z") * lax.axis_size("core")
    y_size, z_size = lax.axis_size("y"), lax.axis_size("z")

    with jax.named_scope("expert_weights"):
        packed = call(
            pack_kernel,
            jax.ShapeDtypeStruct((QUARTER, PACKED), BF16),
            (w_gate, w_up, w_down),
            scratch=[
                pltpu.VMEM((3, QUARTER, QUARTER), BF16),
                pltpu.VMEM((QUARTER, PACKED), BF16),
                pltpu.SemaphoreType.DMA((9,)),
                pltpu.SemaphoreType.DMA((3,)),
            ],
            spaces=[pltpu.HBM] * 3,
            made=pltpu.HBM,
            limit=60,
        )
        weights = lax.all_gather(packed, "tp", axis=0, tiled=False)
        packed, w_out, keys = lax.optimization_barrier((packed, w_out, keys))

    with jax.named_scope("projection_rows"):
        spread = jnp.broadcast_to(w_out[None], (z_size,) + w_out.shape)
        column = lax.all_to_all(spread, "z", 0, 0, tiled=True)
        column = column.reshape(z_size * w_out.shape[0], QUARTER)

    with jax.named_scope("attention"):
        pair = jnp.concatenate([keys, values], axis=1)
        before = lax.ppermute(pair, SEQ, [(i, i + 1) for i in range(seq_size - 1)])
        start = (session_start - seq_index * count + WINDOW)[:, None]
        heads = call(
            attention_kernel,
            jax.ShapeDtypeStruct((2, TP, 2, count, GROUPS * HALF), BF16),
            (queries, pair, before, start, sinks),
            spaces=[pltpu.VMEM] * 4 + [pltpu.SMEM],
            flops=2_000_000_000,
            moved=2_000_000,
            limit=24,
        )
        column, heads = lax.optimization_barrier((column, heads))

    with jax.named_scope("projection_rows"):
        half = column.shape[0] // 2
        ahead, behind, pieces = column, column, [column]
        for _ in range(y_size // 2 - 1):
            ahead, behind = shifted(ahead, "y", 1), shifted(behind, "y", -1)
            pieces += [ahead, behind]
        pieces += [shifted(ahead[:half], "y", 1), shifted(behind[half:], "y", -1)]
        sources = [y]
        for k in range(1, y_size // 2):
            sources += [(y - k) % y_size, (y + k) % y_size]
        sources.append((y + y_size // 2) % y_size)
        index = jnp.stack([jnp.asarray(v, jnp.int32) for v in sources + [core]])

    with jax.named_scope("attention"):
        heads = lax.all_to_all(
            heads.reshape(2 * TP, 2, count, GROUPS * HALF), ("core", "tp"), 0, 0, tiled=True
        )
        heads = heads.reshape(2, TP * 2, count, GROUPS * HALF)

    with jax.named_scope("stream"):
        own, other = call(
            projection_kernel,
            [jax.ShapeDtypeStruct((count, QUARTER), F32)] * 2,
            (index, heads, *pieces),
            scratch=[pltpu.VMEM((2, count, QUARTER), F32)],
            spaces=[pltpu.SMEM] + [pltpu.VMEM] * 10,
            flops=800_000_000,
            moved=4_000_000,
        )
        got = shifted(other, "core", 1)
        stream, scaled = call(
            stream_kernel,
            [
                jax.ShapeDtypeStruct((count, QUARTER), F32),
                jax.ShapeDtypeStruct((count, PADDED), BF16),
            ],
            (residual, own, got, norm_gain[None, :]),
        )

    with jax.named_scope("routing"):
        present = expert_ids[:, :, None] == jnp.arange(EXPERTS, dtype=jnp.int32)[None, None, :]
        per_row = jnp.sum(present.astype(jnp.int32), axis=1)
        earlier = jnp.cumsum(per_row, axis=0) - per_row
        position = jnp.sum(jnp.where(present, earlier[:, None, :], 0), axis=2)
        target = (position // TP) * TARGETS + expert_ids * TP + position % TP
        slots = jnp.arange(CLASS_SLOTS * TARGETS, dtype=jnp.int32)
        routing = jnp.sum((slots[:, None, None] == target[None]).astype(BF16), axis=2)
        mixing = jnp.sum(
            jnp.where(
                slots[None, :, None] == target[:, None, :],
                expert_gates[:, None, :],
                jnp.zeros((), BF16),
            ),
            axis=2,
        )

    flat_scratch = pltpu.VMEM((TARGETS * CHUNK, 128), F32)
    flat_shape = jax.ShapeDtypeStruct((TARGETS * CHUNK, 128), BF16)

    def exchanged(block):
        block = block.reshape(TARGETS, CHUNK // 2, 2, 128)
        return lax.all_to_all(block, PLANE, 0, 0, tiled=True).reshape(flat_shape.shape)

    with jax.named_scope("dispatch"):
        sending = call(
            dispatch_kernel, flat_shape, (scaled, routing), scratch=[flat_scratch], limit=16
        )
        arrived = exchanged(sending)
        partner = shifted(arrived, "core", 1)

    with jax.named_scope("experts"):
        rows, scale = call(
            rows_kernel,
            [
                jax.ShapeDtypeStruct((TP, 2 * SLOTS, PADDED), BF16),
                jax.ShapeDtypeStruct((2 * SLOTS, 1), F32),
            ],
            (arrived, partner),
            scratch=[flat_scratch],
            limit=16,
        )
        to_mine, to_other = call(
            expert_kernel,
            [flat_shape] * 2,
            (rows, scale, weights),
            scratch=[
                flat_scratch,
                pltpu.VMEM((TP, 2 * SLOTS, PADDED), BF16),
                pltpu.VMEM((TP, QUARTER, PACKED), BF16),
                pltpu.SemaphoreType.DMA((2 * TP,)),
            ],
            spaces=[pltpu.HBM, pltpu.VMEM, pltpu.HBM],
            flops=5_000_000_000,
            moved=15_000_000,
            limit=48,
        )
        received = shifted(to_other, "core", 1)
        both = (to_mine.astype(F32) + received.astype(F32)).astype(BF16)

    with jax.named_scope("combine"):
        back = exchanged(both)
        return call(
            combine_kernel,
            jax.ShapeDtypeStruct((count, QUARTER), BF16),
            (back, mixing, stream),
            scratch=[flat_scratch],
            limit=16,
        )


def solution(mesh):
    whole = Mesh(mesh.devices.reshape(8, 8, 2, 4), ("y", "z", "core", "tp"))
    return jax.shard_map(
        shards,
        mesh=whole,
        in_specs=(
            P(SEQ, "tp"),
            P(SEQ, "tp"),
            P(SEQ, "tp"),
            P("tp"),
            P(SEQ),
            P(SEQ, "tp"),
            P(SEQ, "tp"),
            P("tp"),
            P(SEQ, None),
            P(SEQ, None),
            P("tp", SEQ),
            P("tp", SEQ),
            P(SEQ, "tp"),
        ),
        out_specs=P(SEQ, "tp"),
        check_vma=False,
    )
```

```python
import jax
import jax.numpy as jnp
from jax import lax
from jax.experimental import pallas as pl
from jax.experimental.pallas import tpu as pltpu
from jax.sharding import Mesh, PartitionSpec as P

D = 2880
HEAD = 64
HALF = 32
GROUPS = 8
WINDOW = 128
EXPERTS = 64
TP = 4
QUARTER = 720
PADDED = 768
MAIN = 640
TAIL = 80
PACKED = 3 * MAIN + 2 * 128
CHUNK = 18
TARGETS = EXPERTS * TP
CLASS_SLOTS = 3
SLOTS = EXPERTS * CLASS_SLOTS
EPSILON = 1e-05
NEGATIVE = -1e30
F32 = jnp.float32
BF16 = jnp.bfloat16
SEQ = ("y", "z", "core")
PLANE = ("y", "z", "tp")


def shifted(block, axis, distance):
    size = lax.axis_size(axis)
    return lax.ppermute(block, axis, [(i, (i + distance) % size) for i in range(size)])


def call(kernel, out_shape, args, scratch=(), spaces=None, flops=0, moved=0, limit=32, made=pltpu.VMEM):
    spaces = spaces or [pltpu.VMEM] * len(args)
    return pl.pallas_call(
        kernel,
        out_shape=out_shape,
        in_specs=[pl.BlockSpec(memory_space=s) for s in spaces],
        out_specs=jax.tree.map(lambda _: pl.BlockSpec(memory_space=made), out_shape),
        scratch_shapes=list(scratch),
        cost_estimate=pl.CostEstimate(flops=flops, bytes_accessed=moved, transcendentals=0),
        compiler_params=pltpu.CompilerParams(vmem_limit_bytes=limit * 1024 * 1024),
    )(*args)


def attention_kernel(q_ref, own_ref, before_ref, start_ref, sink_ref, out_ref):
    rows = q_ref.shape[0]
    i = lax.broadcasted_iota(jnp.int32, (rows, rows), 0)
    j = lax.broadcasted_iota(jnp.int32, (rows, rows), 1)
    start = start_ref[...]
    allowed_before = (j > i) & (j >= start)
    allowed_own = (j <= i) & (j + WINDOW >= start)
    row = lax.broadcasted_iota(jnp.int32, (2 * HEAD, GROUPS * HALF), 0)
    col = lax.broadcasted_iota(jnp.int32, (2 * HEAD, GROUPS * HALF), 1)
    group_of_lane = lax.broadcasted_iota(jnp.int32, (rows, GROUPS * HALF), 1) // HALF
    contract = (((1,), (1,)), ((), ()))
    for h in range(2):
        lanes = slice(h * HEAD, (h + 1) * HEAD)
        k_own, k_before = own_ref[:, lanes], before_ref[:, lanes]
        spread = []
        for c in range(2):
            pick = (row == h * HEAD + c * HALF + col % HALF).astype(BF16)
            spread.append(
                [
                    jnp.dot(ref[:, 2 * HEAD :], pick, preferred_element_type=F32).astype(BF16)
                    for ref in (before_ref, own_ref)
                ]
            )
        totals = [jnp.zeros((rows, GROUPS * HALF), F32) for _ in range(2)]
        for g in range(GROUPS):
            head = h * GROUPS + g
            q = q_ref[:, head * HEAD : (head + 1) * HEAD]
            s_before = lax.dot_general(q, k_before, contract, preferred_element_type=F32)
            s_own = lax.dot_general(q, k_own, contract, preferred_element_type=F32)
            s_before = jnp.where(allowed_before, s_before * HEAD**-0.5, NEGATIVE)
            s_own = jnp.where(allowed_own, s_own * HEAD**-0.5, NEGATIVE)
            sink = sink_ref[head]
            top = jnp.max(jnp.maximum(s_before, s_own), axis=1, keepdims=True)
            top = jnp.maximum(top, sink)
            e_before = jnp.exp(s_before - top)
            e_own = jnp.exp(s_own - top)
            total = jnp.sum(e_before + e_own, axis=1, keepdims=True) + jnp.exp(sink - top)
            p_before = (e_before / total).astype(BF16)
            p_own = (e_own / total).astype(BF16)
            for c in range(2):
                v_before, v_own = spread[c]
                zero = jnp.zeros_like(v_own)
                mine = group_of_lane == g
                totals[c] += jnp.dot(
                    p_before, jnp.where(mine, v_before, zero), preferred_element_type=F32
                ) + jnp.dot(p_own, jnp.where(mine, v_own, zero), preferred_element_type=F32)
        for c in range(2):
            made = totals[c].astype(BF16)
            for t in range(TP):
                out_ref[c, t, h] = made


def projection_kernel(index_ref, heads_ref, *refs):
    shards, (own_ref, other_ref, total, sems) = refs[:9], refs[9:]
    me = index_ref[8]
    leaving = []
    for n, (half, ref) in enumerate(((1 - me, other_ref), (me, own_ref))):
        acc = jnp.zeros(total.shape[1:], F32)
        for k in range(7):
            chunk = heads_ref[half, index_ref[k]]
            acc += jnp.dot(chunk, shards[k][...], preferred_element_type=F32)
        chunk = heads_ref[half, index_ref[7]]
        depth = chunk.shape[1] // 2
        acc += jnp.dot(chunk[:, :depth], shards[7][...], preferred_element_type=F32)
        acc += jnp.dot(chunk[:, depth:], shards[8][...], preferred_element_type=F32)
        total[n] = acc
        leaving.append(pltpu.make_async_copy(total.at[n], ref, sems.at[n]))
        leaving[n].start()
    for copy in leaving:
        copy.wait()


def stream_kernel(residual_ref, own_ref, got_ref, gain_ref, stream_ref, rows_ref):
    stream = residual_ref[...].astype(F32) + (own_ref[...] + got_ref[...])
    stream_ref[...] = stream
    squares = jnp.sum(stream * stream, axis=1, keepdims=True)
    scaled = (stream * gain_ref[...]).astype(BF16)
    lane = lax.broadcasted_iota(jnp.int32, (stream.shape[0], PADDED - QUARTER), 1)
    high = squares.astype(BF16).astype(F32)
    middle = (squares - high).astype(BF16).astype(F32)
    low = squares - high - middle
    extra = jnp.where(lane == 0, high, jnp.where(lane == 1, middle, jnp.where(lane == 2, low, 0.0)))
    extra = extra.astype(BF16)
    rows_ref[:, :QUARTER] = scaled
    rows_ref[:, QUARTER:] = extra


def dispatch_kernel(rows_ref, routing_ref, out_ref, flat):
    picked = jnp.dot(routing_ref[...], rows_ref[...], preferred_element_type=F32)
    for k in range(CLASS_SLOTS):
        for b in range(6):
            flat[pl.ds(k * 6 + b, TARGETS, stride=CHUNK), :] = picked[
                k * TARGETS : (k + 1) * TARGETS, b * 128 : (b + 1) * 128
            ]
    out_ref[...] = flat[...].astype(BF16)


def pack_kernel(gate_ref, up_ref, down_ref, out_ref, held, made, in_sems, out_sems):
    refs = (gate_ref, up_ref, down_ref)
    span = QUARTER // 3
    arriving, leaving = [], []
    for k in range(3):
        rows = pl.ds(k * span, span)
        for n, ref in enumerate(refs):
            arriving.append(
                pltpu.make_async_copy(ref.at[rows], held.at[n, rows], in_sems.at[3 * k + n])
            )
            arriving[-1].start()
        leaving.append(pltpu.make_async_copy(made.at[rows], out_ref.at[rows], out_sems.at[k]))
    for k in range(3):
        rows = slice(k * span, (k + 1) * span)
        tails = []
        for n in range(3):
            arriving[3 * k + n].wait()
            made[rows, n * MAIN : (n + 1) * MAIN] = held[n, rows, :MAIN]
            tails.append(held[n, rows, MAIN:])
        tails.append(jnp.zeros((span, 2 * 128 - 3 * TAIL), BF16))
        made[rows, 3 * MAIN :] = jnp.concatenate(tails, axis=1)
        leaving[k].start()
    for copy in leaving:
        copy.wait()


def expert_kernel(
    mine_ref, other_ref, weights_ref, to_mine_ref, to_other_ref, flat, rows, w, sems
):
    copies = [pltpu.make_async_copy(weights_ref.at[t], w.at[t], sems.at[t]) for t in range(TP)]
    for copy in copies:
        copy.start()
    squares = []
    for n, ref in enumerate((mine_ref, other_ref)):
        flat[...] = ref[...].astype(F32)
        for k in range(CLASS_SLOTS):
            part = slice(n * SLOTS + k * EXPERTS, n * SLOTS + (k + 1) * EXPERTS)
            total = jnp.zeros((EXPERTS, 1), F32)
            for t in range(TP):
                for b in range(6):
                    piece = flat[pl.ds(t * CHUNK + k * 6 + b, EXPERTS, stride=TP * CHUNK), :]
                    rows[t, part, b * 128 : (b + 1) * 128] = piece.astype(BF16)
                lane = lax.broadcasted_iota(jnp.int32, piece.shape, 1)
                total += jnp.sum(jnp.where(lane >= TAIL, piece, 0.0), axis=1, keepdims=True)
            squares.append(total)
    scale = lax.rsqrt(jnp.concatenate(squares, axis=0) / D + EPSILON)
    sums = jnp.zeros((2 * SLOTS, 2 * MAIN), F32)
    ends = jnp.zeros((2 * SLOTS, 2 * 128), F32)
    for t in range(TP):
        copies[t].wait()
        part = rows[t, :, :QUARTER]
        sums += jnp.dot(part, w[t, :, : 2 * MAIN], preferred_element_type=F32)
        ends += jnp.dot(part, w[t, :, 3 * MAIN :], preferred_element_type=F32)
    gate = jnp.concatenate([sums[:, :MAIN], ends[:, :TAIL]], axis=1) * scale
    up = jnp.concatenate([sums[:, MAIN:], ends[:, TAIL : 2 * TAIL]], axis=1) * scale
    active = (gate / (1.0 + jnp.exp(-gate)) * up).astype(BF16)
    for n, ref in enumerate((to_mine_ref, to_other_ref)):
        part = active[n * SLOTS : (n + 1) * SLOTS]
        for t in range(TP):
            made = jnp.dot(part, w[t, :, 2 * MAIN : 3 * MAIN], preferred_element_type=F32)
            last = jnp.dot(part, w[t, :, 3 * MAIN :], preferred_element_type=F32)
            last = jnp.concatenate(
                [last[:, 2 * TAIL : 3 * TAIL], jnp.zeros((SLOTS, 128 - TAIL), F32)], axis=1
            )
            for k in range(CLASS_SLOTS):
                group = slice(k * EXPERTS, (k + 1) * EXPERTS)
                for b in range(6):
                    piece = made[group, b * 128 : (b + 1) * 128] if b < 5 else last[group]
                    flat[pl.ds(t * CHUNK + k * 6 + b, EXPERTS, stride=TP * CHUNK), :] = piece
        ref[...] = flat[...].astype(BF16)


def combine_kernel(back_ref, mixing_ref, stream_ref, out_ref, flat):
    flat[...] = back_ref[...].astype(F32)
    for b in range(6):
        total = jnp.zeros((out_ref.shape[0], 128), F32)
        for k in range(CLASS_SLOTS):
            part = flat[pl.ds(k * 6 + b, TARGETS, stride=CHUNK), :].astype(BF16)
            total += jnp.dot(
                mixing_ref[:, k * TARGETS : (k + 1) * TARGETS], part, preferred_element_type=F32
            )
        width = min(128, QUARTER - b * 128)
        lanes = slice(b * 128, b * 128 + width)
        out_ref[:, lanes] = (stream_ref[:, lanes] + total[:, :width]).astype(BF16)


def shards(
    queries,
    keys,
    values,
    sinks,
    session_start,
    residual,
    w_out,
    norm_gain,
    expert_ids,
    expert_gates,
    w_gate,
    w_up,
    w_down,
):
    count = queries.shape[0]
    y, core, tp = lax.axis_index("y"), lax.axis_index("core"), lax.axis_index("tp")
    seq_index = lax.axis_index(SEQ)
    seq_size = lax.axis_size("y") * lax.axis_size("z") * lax.axis_size("core")
    y_size, z_size = lax.axis_size("y"), lax.axis_size("z")

    with jax.named_scope("expert_weights"):
        packed = call(
            pack_kernel,
            jax.ShapeDtypeStruct((QUARTER, PACKED), BF16),
            (w_gate, w_up, w_down),
            scratch=[
                pltpu.VMEM((3, QUARTER, QUARTER), BF16),
                pltpu.VMEM((QUARTER, PACKED), BF16),
                pltpu.SemaphoreType.DMA((9,)),
                pltpu.SemaphoreType.DMA((3,)),
            ],
            spaces=[pltpu.HBM] * 3,
            made=pltpu.HBM,
            limit=60,
        )
        weights = lax.all_gather(packed, "tp", axis=0, tiled=False)
        packed, w_out, keys = lax.optimization_barrier((packed, w_out, keys))

    with jax.named_scope("projection_rows"):
        spread = jnp.broadcast_to(w_out[None], (z_size,) + w_out.shape)
        column = lax.all_to_all(spread, "z", 0, 0, tiled=True)
        column = column.reshape(z_size * w_out.shape[0], QUARTER)

    with jax.named_scope("attention"):
        pair = jnp.concatenate([keys, values], axis=1)
        before = lax.ppermute(pair, SEQ, [(i, i + 1) for i in range(seq_size - 1)])
        start = (session_start - seq_index * count + WINDOW)[:, None]
        heads = call(
            attention_kernel,
            jax.ShapeDtypeStruct((2, TP, 2, count, GROUPS * HALF), BF16),
            (queries, pair, before, start, sinks),
            spaces=[pltpu.VMEM] * 4 + [pltpu.SMEM],
            flops=2_000_000_000,
            moved=2_000_000,
            limit=24,
        )
        column, heads = lax.optimization_barrier((column, heads))

    with jax.named_scope("projection_rows"):
        half = column.shape[0] // 2
        ahead, behind, pieces = column, column, [column]
        for _ in range(y_size // 2 - 1):
            ahead, behind = shifted(ahead, "y", 1), shifted(behind, "y", -1)
            pieces += [ahead, behind]
        pieces += [shifted(ahead[:half], "y", 1), shifted(behind[half:], "y", -1)]
        sources = [y]
        for k in range(1, y_size // 2):
            sources += [(y - k) % y_size, (y + k) % y_size]
        sources.append((y + y_size // 2) % y_size)
        index = jnp.stack([jnp.asarray(v, jnp.int32) for v in sources + [core]])

    with jax.named_scope("attention"):
        heads = lax.all_to_all(
            heads.reshape(2 * TP, 2, count, GROUPS * HALF), ("core", "tp"), 0, 0, tiled=True
        )
        heads = heads.reshape(2, TP * 2, count, GROUPS * HALF)

    with jax.named_scope("stream"):
        own, other = call(
            projection_kernel,
            [jax.ShapeDtypeStruct((count, QUARTER), F32)] * 2,
            (index, heads, *pieces),
            scratch=[pltpu.VMEM((2, count, QUARTER), F32), pltpu.SemaphoreType.DMA((2,))],
            made=pltpu.HBM,
            spaces=[pltpu.SMEM] + [pltpu.VMEM] * 10,
            flops=800_000_000,
            moved=4_000_000,
        )
        got = shifted(other, "core", 1)
        stream, scaled = call(
            stream_kernel,
            [
                jax.ShapeDtypeStruct((count, QUARTER), F32),
                jax.ShapeDtypeStruct((count, PADDED), BF16),
            ],
            (residual, own, got, norm_gain[None, :]),
        )

    with jax.named_scope("routing"):
        present = expert_ids[:, :, None] == jnp.arange(EXPERTS, dtype=jnp.int32)[None, None, :]
        per_row = jnp.sum(present.astype(jnp.int32), axis=1)
        earlier = jnp.cumsum(per_row, axis=0) - per_row
        position = jnp.sum(jnp.where(present, earlier[:, None, :], 0), axis=2)
        target = (position // TP) * TARGETS + expert_ids * TP + position % TP
        slots = jnp.arange(CLASS_SLOTS * TARGETS, dtype=jnp.int32)
        routing = jnp.sum((slots[:, None, None] == target[None]).astype(BF16), axis=2)
        mixing = jnp.sum(
            jnp.where(
                slots[None, :, None] == target[:, None, :],
                expert_gates[:, None, :],
                jnp.zeros((), BF16),
            ),
            axis=2,
        )

    flat_scratch = pltpu.VMEM((TARGETS * CHUNK, 128), F32)
    flat_shape = jax.ShapeDtypeStruct((TARGETS * CHUNK, 128), BF16)

    def exchanged(block):
        block = block.reshape(TARGETS, CHUNK // 2, 2, 128)
        return lax.all_to_all(block, PLANE, 0, 0, tiled=True).reshape(flat_shape.shape)

    with jax.named_scope("dispatch"):
        sending = call(
            dispatch_kernel, flat_shape, (scaled, routing), scratch=[flat_scratch], limit=16
        )
        arrived = exchanged(sending)
        partner = shifted(arrived, "core", 1)

    with jax.named_scope("experts"):
        to_mine, to_other = call(
            expert_kernel,
            [flat_shape] * 2,
            (arrived, partner, weights),
            scratch=[
                flat_scratch,
                pltpu.VMEM((TP, 2 * SLOTS, PADDED), BF16),
                pltpu.VMEM((TP, QUARTER, PACKED), BF16),
                pltpu.SemaphoreType.DMA((TP,)),
            ],
            spaces=[pltpu.VMEM] * 2 + [pltpu.HBM],
            flops=5_000_000_000,
            moved=15_000_000,
            limit=48,
        )
        received = shifted(to_other, "core", 1)
        both = (to_mine.astype(F32) + received.astype(F32)).astype(BF16)

    with jax.named_scope("combine"):
        back = exchanged(both)
        return call(
            combine_kernel,
            jax.ShapeDtypeStruct((count, QUARTER), BF16),
            (back, mixing, stream),
            scratch=[flat_scratch],
            limit=16,
        )


def solution(mesh):
    whole = Mesh(mesh.devices.reshape(8, 8, 2, 4), ("y", "z", "core", "tp"))
    return jax.shard_map(
        shards,
        mesh=whole,
        in_specs=(
            P(SEQ, "tp"),
            P(SEQ, "tp"),
            P(SEQ, "tp"),
            P("tp"),
            P(SEQ),
            P(SEQ, "tp"),
            P(SEQ, "tp"),
            P("tp"),
            P(SEQ, None),
            P(SEQ, None),
            P("tp", SEQ),
            P("tp", SEQ),
            P(SEQ, "tp"),
        ),
        out_specs=P(SEQ, "tp"),
        check_vma=False,
    )
```

```python
import jax
import jax.numpy as jnp
from jax import lax
from jax.experimental import pallas as pl
from jax.experimental.pallas import tpu as pltpu
from jax.sharding import Mesh, PartitionSpec as P

D = 2880
HEAD = 64
HALF = 32
GROUPS = 8
WINDOW = 128
EXPERTS = 64
TP = 4
QUARTER = 720
PADDED = 768
MAIN = 640
TAIL = 80
PACKED = 3 * MAIN + 2 * 128
CHUNK = 18
TARGETS = EXPERTS * TP
CLASS_SLOTS = 3
SLOTS = EXPERTS * CLASS_SLOTS
EPSILON = 1e-05
NEGATIVE = -1e30
F32 = jnp.float32
BF16 = jnp.bfloat16
SEQ = ("y", "z", "core")
PLANE = ("y", "z", "tp")


def shifted(block, axis, distance):
    size = lax.axis_size(axis)
    return lax.ppermute(block, axis, [(i, (i + distance) % size) for i in range(size)])


def call(kernel, out_shape, args, scratch=(), spaces=None, flops=0, moved=0, limit=32, made=pltpu.VMEM):
    spaces = spaces or [pltpu.VMEM] * len(args)
    return pl.pallas_call(
        kernel,
        out_shape=out_shape,
        in_specs=[pl.BlockSpec(memory_space=s) for s in spaces],
        out_specs=jax.tree.map(lambda _: pl.BlockSpec(memory_space=made), out_shape),
        scratch_shapes=list(scratch),
        cost_estimate=pl.CostEstimate(flops=flops, bytes_accessed=moved, transcendentals=0),
        compiler_params=pltpu.CompilerParams(vmem_limit_bytes=limit * 1024 * 1024),
    )(*args)


def attention_kernel(q_ref, own_ref, before_ref, start_ref, sink_ref, out_ref):
    rows = q_ref.shape[0]
    i = lax.broadcasted_iota(jnp.int32, (rows, rows), 0)
    j = lax.broadcasted_iota(jnp.int32, (rows, rows), 1)
    start = start_ref[...]
    allowed_before = (j > i) & (j >= start)
    allowed_own = (j <= i) & (j + WINDOW >= start)
    row = lax.broadcasted_iota(jnp.int32, (2 * HEAD, GROUPS * HALF), 0)
    col = lax.broadcasted_iota(jnp.int32, (2 * HEAD, GROUPS * HALF), 1)
    group_of_lane = lax.broadcasted_iota(jnp.int32, (rows, GROUPS * HALF), 1) // HALF
    contract = (((1,), (1,)), ((), ()))
    for h in range(2):
        lanes = slice(h * HEAD, (h + 1) * HEAD)
        k_own, k_before = own_ref[:, lanes], before_ref[:, lanes]
        spread = []
        for c in range(2):
            pick = (row == h * HEAD + c * HALF + col % HALF).astype(BF16)
            spread.append(
                [
                    jnp.dot(ref[:, 2 * HEAD :], pick, preferred_element_type=F32).astype(BF16)
                    for ref in (before_ref, own_ref)
                ]
            )
        totals = [jnp.zeros((rows, GROUPS * HALF), F32) for _ in range(2)]
        for g in range(GROUPS):
            head = h * GROUPS + g
            q = q_ref[:, head * HEAD : (head + 1) * HEAD]
            s_before = lax.dot_general(q, k_before, contract, preferred_element_type=F32)
            s_own = lax.dot_general(q, k_own, contract, preferred_element_type=F32)
            s_before = jnp.where(allowed_before, s_before * HEAD**-0.5, NEGATIVE)
            s_own = jnp.where(allowed_own, s_own * HEAD**-0.5, NEGATIVE)
            sink = sink_ref[head]
            top = jnp.max(jnp.maximum(s_before, s_own), axis=1, keepdims=True)
            top = jnp.maximum(top, sink)
            e_before = jnp.exp(s_before - top)
            e_own = jnp.exp(s_own - top)
            total = jnp.sum(e_before + e_own, axis=1, keepdims=True) + jnp.exp(sink - top)
            p_before = (e_before / total).astype(BF16)
            p_own = (e_own / total).astype(BF16)
            for c in range(2):
                v_before, v_own = spread[c]
                zero = jnp.zeros_like(v_own)
                mine = group_of_lane == g
                totals[c] += jnp.dot(
                    p_before, jnp.where(mine, v_before, zero), preferred_element_type=F32
                ) + jnp.dot(p_own, jnp.where(mine, v_own, zero), preferred_element_type=F32)
        for c in range(2):
            made = totals[c].astype(BF16)
            for t in range(TP):
                out_ref[c, t, h] = made


def projection_kernel(index_ref, heads_ref, *refs):
    shards, (own_ref, other_ref, total, sems) = refs[:9], refs[9:]
    me = index_ref[8]
    leaving = []
    for n, (half, ref) in enumerate(((1 - me, other_ref), (me, own_ref))):
        acc = jnp.zeros(total.shape[1:], F32)
        for k in range(7):
            chunk = heads_ref[half, index_ref[k]]
            acc += jnp.dot(chunk, shards[k][...], preferred_element_type=F32)
        chunk = heads_ref[half, index_ref[7]]
        depth = chunk.shape[1] // 2
        acc += jnp.dot(chunk[:, :depth], shards[7][...], preferred_element_type=F32)
        acc += jnp.dot(chunk[:, depth:], shards[8][...], preferred_element_type=F32)
        total[n] = acc
        leaving.append(pltpu.make_async_copy(total.at[n], ref, sems.at[n]))
        leaving[n].start()
    for copy in leaving:
        copy.wait()


def stream_kernel(residual_ref, own_ref, got_ref, gain_ref, stream_ref, rows_ref):
    stream = residual_ref[...].astype(F32) + (own_ref[...] + got_ref[...])
    stream_ref[...] = stream
    squares = jnp.sum(stream * stream, axis=1, keepdims=True)
    scaled = (stream * gain_ref[...]).astype(BF16)
    lane = lax.broadcasted_iota(jnp.int32, (stream.shape[0], PADDED - QUARTER), 1)
    high = squares.astype(BF16).astype(F32)
    middle = (squares - high).astype(BF16).astype(F32)
    low = squares - high - middle
    extra = jnp.where(lane == 0, high, jnp.where(lane == 1, middle, jnp.where(lane == 2, low, 0.0)))
    extra = extra.astype(BF16)
    rows_ref[:, :QUARTER] = scaled
    rows_ref[:, QUARTER:] = extra


def dispatch_kernel(rows_ref, routing_ref, out_ref, flat):
    picked = jnp.dot(routing_ref[...], rows_ref[...], preferred_element_type=F32)
    for k in range(CLASS_SLOTS):
        for b in range(6):
            flat[pl.ds(k * 6 + b, TARGETS, stride=CHUNK), :] = picked[
                k * TARGETS : (k + 1) * TARGETS, b * 128 : (b + 1) * 128
            ]
    out_ref[...] = flat[...].astype(BF16)


def pack_kernel(gate_ref, up_ref, down_ref, out_ref, held, made, in_sems, out_sems):
    refs = (gate_ref, up_ref, down_ref)
    span = QUARTER // 3
    arriving, leaving = [], []
    for k in range(3):
        rows = pl.ds(k * span, span)
        for n, ref in enumerate(refs):
            arriving.append(
                pltpu.make_async_copy(ref.at[rows], held.at[n, rows], in_sems.at[3 * k + n])
            )
            arriving[-1].start()
        leaving.append(pltpu.make_async_copy(made.at[rows], out_ref.at[rows], out_sems.at[k]))
    for k in range(3):
        rows = slice(k * span, (k + 1) * span)
        tails = []
        for n in range(3):
            arriving[3 * k + n].wait()
            made[rows, n * MAIN : (n + 1) * MAIN] = held[n, rows, :MAIN]
            tails.append(held[n, rows, MAIN:])
        tails.append(jnp.zeros((span, 2 * 128 - 3 * TAIL), BF16))
        made[rows, 3 * MAIN :] = jnp.concatenate(tails, axis=1)
        leaving[k].start()
    for copy in leaving:
        copy.wait()


def give_back(part, main_of, ends_of, flat):
    for t in range(TP):
        made = jnp.dot(part, main_of(t), preferred_element_type=F32)
        last = jnp.dot(part, ends_of(t), preferred_element_type=F32)
        last = jnp.concatenate(
            [last[:, 2 * TAIL : 3 * TAIL], jnp.zeros((SLOTS, 128 - TAIL), F32)], axis=1
        )
        for k in range(CLASS_SLOTS):
            group = slice(k * EXPERTS, (k + 1) * EXPERTS)
            for b in range(6):
                piece = made[group, b * 128 : (b + 1) * 128] if b < 5 else last[group]
                flat[pl.ds(t * CHUNK + k * 6 + b, EXPERTS, stride=TP * CHUNK), :] = piece


def down_kernel(active_ref, weights_ref, out_ref, flat, w, sems):
    columns = pl.ds(2 * MAIN, PACKED - 2 * MAIN)
    copies = [
        pltpu.make_async_copy(weights_ref.at[t, :, columns], w.at[t], sems.at[t])
        for t in range(TP)
    ]
    for copy in copies:
        copy.start()
    for copy in copies:
        copy.wait()
    give_back(active_ref[...], lambda t: w[t, :, :MAIN], lambda t: w[t, :, MAIN:], flat)
    out_ref[...] = flat[...].astype(BF16)


def expert_kernel(
    mine_ref, other_ref, weights_ref, active_ref, to_other_ref, flat, rows, w, sems
):
    copies = [pltpu.make_async_copy(weights_ref.at[t], w.at[t], sems.at[t]) for t in range(TP)]
    for copy in copies:
        copy.start()
    squares = []
    for n, ref in enumerate((mine_ref, other_ref)):
        flat[...] = ref[...].astype(F32)
        for k in range(CLASS_SLOTS):
            part = slice(n * SLOTS + k * EXPERTS, n * SLOTS + (k + 1) * EXPERTS)
            total = jnp.zeros((EXPERTS, 1), F32)
            for t in range(TP):
                for b in range(6):
                    piece = flat[pl.ds(t * CHUNK + k * 6 + b, EXPERTS, stride=TP * CHUNK), :]
                    rows[t, part, b * 128 : (b + 1) * 128] = piece.astype(BF16)
                lane = lax.broadcasted_iota(jnp.int32, piece.shape, 1)
                total += jnp.sum(jnp.where(lane >= TAIL, piece, 0.0), axis=1, keepdims=True)
            squares.append(total)
    scale = lax.rsqrt(jnp.concatenate(squares, axis=0) / D + EPSILON)
    sums = jnp.zeros((2 * SLOTS, 2 * MAIN), F32)
    ends = jnp.zeros((2 * SLOTS, 2 * 128), F32)
    for t in range(TP):
        copies[t].wait()
        part = rows[t, :, :QUARTER]
        sums += jnp.dot(part, w[t, :, : 2 * MAIN], preferred_element_type=F32)
        ends += jnp.dot(part, w[t, :, 3 * MAIN :], preferred_element_type=F32)
    gate = jnp.concatenate([sums[:, :MAIN], ends[:, :TAIL]], axis=1) * scale
    up = jnp.concatenate([sums[:, MAIN:], ends[:, TAIL : 2 * TAIL]], axis=1) * scale
    active = (gate / (1.0 + jnp.exp(-gate)) * up).astype(BF16)
    active_ref[...] = active[:SLOTS]
    give_back(
        active[SLOTS:],
        lambda t: w[t, :, 2 * MAIN : 3 * MAIN],
        lambda t: w[t, :, 3 * MAIN :],
        flat,
    )
    to_other_ref[...] = flat[...].astype(BF16)


def combine_kernel(back_ref, mixing_ref, stream_ref, out_ref, flat):
    flat[...] = back_ref[...].astype(F32)
    for b in range(6):
        total = jnp.zeros((out_ref.shape[0], 128), F32)
        for k in range(CLASS_SLOTS):
            part = flat[pl.ds(k * 6 + b, TARGETS, stride=CHUNK), :].astype(BF16)
            total += jnp.dot(
                mixing_ref[:, k * TARGETS : (k + 1) * TARGETS], part, preferred_element_type=F32
            )
        width = min(128, QUARTER - b * 128)
        lanes = slice(b * 128, b * 128 + width)
        out_ref[:, lanes] = (stream_ref[:, lanes] + total[:, :width]).astype(BF16)


def shards(
    queries,
    keys,
    values,
    sinks,
    session_start,
    residual,
    w_out,
    norm_gain,
    expert_ids,
    expert_gates,
    w_gate,
    w_up,
    w_down,
):
    count = queries.shape[0]
    y, core, tp = lax.axis_index("y"), lax.axis_index("core"), lax.axis_index("tp")
    seq_index = lax.axis_index(SEQ)
    seq_size = lax.axis_size("y") * lax.axis_size("z") * lax.axis_size("core")
    y_size, z_size = lax.axis_size("y"), lax.axis_size("z")

    with jax.named_scope("expert_weights"):
        packed = call(
            pack_kernel,
            jax.ShapeDtypeStruct((QUARTER, PACKED), BF16),
            (w_gate, w_up, w_down),
            scratch=[
                pltpu.VMEM((3, QUARTER, QUARTER), BF16),
                pltpu.VMEM((QUARTER, PACKED), BF16),
                pltpu.SemaphoreType.DMA((9,)),
                pltpu.SemaphoreType.DMA((3,)),
            ],
            spaces=[pltpu.HBM] * 3,
            made=pltpu.HBM,
            limit=60,
        )
        weights = lax.all_gather(packed, "tp", axis=0, tiled=False)
        packed, w_out, keys = lax.optimization_barrier((packed, w_out, keys))

    with jax.named_scope("projection_rows"):
        spread = jnp.broadcast_to(w_out[None], (z_size,) + w_out.shape)
        column = lax.all_to_all(spread, "z", 0, 0, tiled=True)
        column = column.reshape(z_size * w_out.shape[0], QUARTER)

    with jax.named_scope("attention"):
        pair = jnp.concatenate([keys, values], axis=1)
        before = lax.ppermute(pair, SEQ, [(i, i + 1) for i in range(seq_size - 1)])
        start = (session_start - seq_index * count + WINDOW)[:, None]
        heads = call(
            attention_kernel,
            jax.ShapeDtypeStruct((2, TP, 2, count, GROUPS * HALF), BF16),
            (queries, pair, before, start, sinks),
            spaces=[pltpu.VMEM] * 4 + [pltpu.SMEM],
            flops=2_000_000_000,
            moved=2_000_000,
            limit=24,
        )
        column, heads = lax.optimization_barrier((column, heads))

    with jax.named_scope("projection_rows"):
        half = column.shape[0] // 2
        ahead, behind, pieces = column, column, [column]
        for _ in range(y_size // 2 - 1):
            ahead, behind = shifted(ahead, "y", 1), shifted(behind, "y", -1)
            pieces += [ahead, behind]
        pieces += [shifted(ahead[:half], "y", 1), shifted(behind[half:], "y", -1)]
        sources = [y]
        for k in range(1, y_size // 2):
            sources += [(y - k) % y_size, (y + k) % y_size]
        sources.append((y + y_size // 2) % y_size)
        index = jnp.stack([jnp.asarray(v, jnp.int32) for v in sources + [core]])

    with jax.named_scope("attention"):
        heads = lax.all_to_all(
            heads.reshape(2 * TP, 2, count, GROUPS * HALF), ("core", "tp"), 0, 0, tiled=True
        )
        heads = heads.reshape(2, TP * 2, count, GROUPS * HALF)

    with jax.named_scope("stream"):
        own, other = call(
            projection_kernel,
            [jax.ShapeDtypeStruct((count, QUARTER), F32)] * 2,
            (index, heads, *pieces),
            scratch=[pltpu.VMEM((2, count, QUARTER), F32), pltpu.SemaphoreType.DMA((2,))],
            made=pltpu.HBM,
            spaces=[pltpu.SMEM] + [pltpu.VMEM] * 10,
            flops=800_000_000,
            moved=4_000_000,
        )
        got = shifted(other, "core", 1)
        stream, scaled = call(
            stream_kernel,
            [
                jax.ShapeDtypeStruct((count, QUARTER), F32),
                jax.ShapeDtypeStruct((count, PADDED), BF16),
            ],
            (residual, own, got, norm_gain[None, :]),
        )

    with jax.named_scope("routing"):
        present = expert_ids[:, :, None] == jnp.arange(EXPERTS, dtype=jnp.int32)[None, None, :]
        per_row = jnp.sum(present.astype(jnp.int32), axis=1)
        earlier = jnp.cumsum(per_row, axis=0) - per_row
        position = jnp.sum(jnp.where(present, earlier[:, None, :], 0), axis=2)
        target = (position // TP) * TARGETS + expert_ids * TP + position % TP
        slots = jnp.arange(CLASS_SLOTS * TARGETS, dtype=jnp.int32)
        routing = jnp.sum((slots[:, None, None] == target[None]).astype(BF16), axis=2)
        mixing = jnp.sum(
            jnp.where(
                slots[None, :, None] == target[:, None, :],
                expert_gates[:, None, :],
                jnp.zeros((), BF16),
            ),
            axis=2,
        )

    flat_scratch = pltpu.VMEM((TARGETS * CHUNK, 128), F32)
    flat_shape = jax.ShapeDtypeStruct((TARGETS * CHUNK, 128), BF16)

    def exchanged(block):
        block = block.reshape(TARGETS, CHUNK // 2, 2, 128)
        return lax.all_to_all(block, PLANE, 0, 0, tiled=True).reshape(flat_shape.shape)

    with jax.named_scope("dispatch"):
        sending = call(
            dispatch_kernel, flat_shape, (scaled, routing), scratch=[flat_scratch], limit=16
        )
        arrived = exchanged(sending)
        partner = shifted(arrived, "core", 1)

    with jax.named_scope("experts"):
        active, to_other = call(
            expert_kernel,
            [jax.ShapeDtypeStruct((SLOTS, QUARTER), BF16), flat_shape],
            (arrived, partner, weights),
            scratch=[
                flat_scratch,
                pltpu.VMEM((TP, 2 * SLOTS, PADDED), BF16),
                pltpu.VMEM((TP, QUARTER, PACKED), BF16),
                pltpu.SemaphoreType.DMA((TP,)),
            ],
            spaces=[pltpu.VMEM] * 2 + [pltpu.HBM],
            flops=5_000_000_000,
            moved=15_000_000,
            limit=48,
        )
        received = shifted(to_other, "core", 1)
        to_mine = call(
            down_kernel,
            flat_shape,
            (active, weights),
            scratch=[
                flat_scratch,
                pltpu.VMEM((TP, QUARTER, PACKED - 2 * MAIN), BF16),
                pltpu.SemaphoreType.DMA((TP,)),
            ],
            spaces=[pltpu.VMEM, pltpu.HBM],
            flops=1_000_000_000,
            moved=6_000_000,
            limit=48,
        )
        both = (to_mine.astype(F32) + received.astype(F32)).astype(BF16)

    with jax.named_scope("combine"):
        back = exchanged(both)
        return call(
            combine_kernel,
            jax.ShapeDtypeStruct((count, QUARTER), BF16),
            (back, mixing, stream),
            scratch=[flat_scratch],
            limit=16,
        )


def solution(mesh):
    whole = Mesh(mesh.devices.reshape(8, 8, 2, 4), ("y", "z", "core", "tp"))
    return jax.shard_map(
        shards,
        mesh=whole,
        in_specs=(
            P(SEQ, "tp"),
            P(SEQ, "tp"),
            P(SEQ, "tp"),
            P("tp"),
            P(SEQ),
            P(SEQ, "tp"),
            P(SEQ, "tp"),
            P("tp"),
            P(SEQ, None),
            P(SEQ, None),
            P("tp", SEQ),
            P("tp", SEQ),
            P(SEQ, "tp"),
        ),
        out_specs=P(SEQ, "tp"),
        check_vma=False,
    )
```
